32 devices in a mesh: row: 8 (over y, x, core), col: 4 (over z).
Axes of the slice: x: 2, y: 2, z: 4, core: 2. Of those that a mesh axis runs over, the one named last changes fastest.
Arguments:
- right_side: float32 [4096, 4096], P('row', 'col'), may hold values from -170 to 170, as said below
- kappa_sq: float32 [4096, 4096], P('row', 'col'), may hold values from 0.02 to 0.5
- block_tract: int32 [256, 256], P('row', 'col'), may hold values from 0 to 63
- tract_county: int32 [2048], P(('row', 'col')), may hold values from 0 to 511
- county_state: int32 [512], replicated, may hold values from 0 to 55
- schur: float32 [4, 2048, 8, 1024], P(None, 'row', None, 'col'), may hold values from -64 to 65, as said below
Outputs:
- solution: float32 [4096, 4096], P('row', 'col')
- residual: float32 [4096, 4096], P('row', 'col')
- tract_totals: float32 [2048], P(('row', 'col'))
- county_totals: float32 [512], replicated
- state_totals: float32 [56], replicated
- updated: float32 [4, 2048, 8, 1024], P(None, 'row', None, 'col')
- panel: float32 [4, 2048, 256], P(None, 'row')
The draws below stay inside these ranges and needn't reach their ends.
Inputs may be any that keep to these rules, and one draw needn't show every extreme that they name: `right_side`: a real field; its size varies strongly between rows, columns and regions. `schur`: symmetric positive definite.
All inputs are finite; a program needn't handle non-finite values.
Results may differ from the reference program's by a relative error of at most 0.0003.
Values sent between devices are 32-bit elements; how exact they have to be, the bound alone decides.
No kernel may reach another device: no remote copies, remote signals or barrier semaphores. Data moves between devices by JAX's collectives and lax.ppermute only.
A program may use at most 128 MiB of HBM per device.

```python
import math
import jax
import jax.numpy as jnp
from jax import lax

CX = 512
CY = 1024
BLOCK = 16
TRACTS_DEV = 64
ITERS = 2
COUNTIES = 512
STATES = 56
NB = 256
ORDER = 8192
NX = 4096
NY = 4096
TRACTS = 2048
RB = 4
CB = 8
N_ROW = 8
N_COL = 4


def draw_right_side(key, part):
    keys = jax.random.split(key, 3)
    row_pos = jnp.arange(NX, dtype=jnp.float32) / max(NX - 1, 1)
    row_scale = jnp.exp(jax.random.uniform(keys[1], (NX,), minval=math.log(0.3), maxval=math.log(3.0)))
    col_scale = jnp.exp(jax.random.uniform(keys[2], (NY,), minval=math.log(0.3), maxval=math.log(3.0)))
    base = jnp.clip(jax.random.normal(keys[0], (NX, NY)), -5.0, 5.0)
    rising = 1.0 + 2.0 * row_pos
    return (base * row_scale[:, None] * col_scale[None, :] * rising[:, None]).astype(jnp.float32)


def draw_schur(key, part):
    keys = jax.random.split(key, 1)
    spread = 2.0 / math.sqrt(NB)
    loading = jnp.clip(jax.random.normal(keys[0], (ORDER, NB)), -4.0, 4.0) * spread
    loading = loading.astype(jnp.float32)
    product = jnp.dot(loading, loading.T, precision=lax.Precision.HIGHEST)
    symmetric = 0.5 * (product + product.T)
    matrix = symmetric + jnp.eye(ORDER, dtype=jnp.float32)
    return matrix.astype(jnp.float32).reshape(RB, ORDER // RB, CB, ORDER // CB)


def place_ends(drawn, own_key, low, top_value):
    shape = drawn.shape
    index_at = [jax.random.randint(jax.random.fold_in(own_key, axis), (), 0, shape[axis]) for axis in range(len(shape))]
    drawn = drawn.at[tuple(index_at)].set(low)
    longest = shape.index(max(shape))
    index_at[longest] = (index_at[longest] + 1) % shape[longest]
    return drawn.at[tuple(index_at)].set(top_value)


def shard_levels(stream_key, dims, cuts, least, high):
    def one(dim, shards_of):
        heights = jax.random.uniform(jax.random.fold_in(jax.random.fold_in(stream_key, 6), dim), (shards_of,), jnp.float32, least / len(cuts), high / len(cuts))
        return jnp.repeat(jnp.exp(heights), dims[dim] // shards_of).reshape((-1,) + (1,) * (len(dims) - dim - 1))

    gain = one(*cuts[0])
    for cut in cuts[1:]:
        gain = gain * one(*cut)
    return gain


def setup_inputs(seed: int = 0) -> dict:
    key_of = jax.random.split(jax.random.key(seed), 7)
    right_side = draw_right_side(jax.random.fold_in(key_of[6], 71), 0)
    kappa_sq = jnp.clip(jnp.exp(math.log(0.5) - 3.218876 * jax.random.uniform(key_of[1], (NX, NY), jnp.float32) ** shard_levels(key_of[1], (NX, NY), ((0, 8), (1, 4)), -0.2, 0.2)), 0.02, 0.5)
    block_tract = place_ends(jax.random.randint(key_of[2], (NX // BLOCK, NY // BLOCK), 0, TRACTS_DEV), jax.random.fold_in(key_of[2], 1), 0, TRACTS_DEV - 1).astype(jnp.int32)
    tract_county = place_ends(jax.random.randint(key_of[3], (TRACTS,), 0, COUNTIES), jax.random.fold_in(key_of[3], 1), 0, COUNTIES - 1).astype(jnp.int32)
    county_state = place_ends(jax.random.randint(key_of[4], (COUNTIES,), 0, STATES), jax.random.fold_in(key_of[4], 1), 0, STATES - 1).astype(jnp.int32)
    schur = draw_schur(jax.random.fold_in(key_of[6], 71), 0)
    return {"right_side": right_side, "kappa_sq": kappa_sq, "block_tract": block_tract, "tract_county": tract_county, "county_state": county_state, "schur": schur}


def apply_rate(grid_field, rate_field):
    padded = jnp.pad(grid_field, 1)
    beside_all = padded[:-2, 1:-1] + padded[2:, 1:-1]
    beside_all = beside_all + padded[1:-1, :-2] + padded[1:-1, 2:]
    return (4.0 + rate_field) * grid_field - beside_all

def precision(grid_field, rate_field):
    return apply_rate(apply_rate(grid_field, rate_field), rate_field)

def reference(right_side, kappa_sq, block_tract, tract_county, county_state, schur):
    solution = jnp.zeros_like(right_side)
    residual = right_side
    direction = right_side
    norm_now = jnp.sum(residual * residual)
    for iteration in range(ITERS):
        applied = precision(direction, kappa_sq)
        step_size = norm_now / jnp.sum(direction * applied)
        solution = solution + step_size * direction
        residual = residual - step_size * applied
        norm_next = jnp.sum(residual * residual)
        direction = residual + norm_next / norm_now * direction
        norm_now = norm_next
    block_sums = solution.reshape(NX // BLOCK, BLOCK, NY // BLOCK, BLOCK).sum(axis=(1, 3))
    block_rows = jnp.arange(NX // BLOCK, dtype=jnp.int32) // (CX // BLOCK)
    block_cols = jnp.arange(NY // BLOCK, dtype=jnp.int32) // (CY // BLOCK)
    tile_index = block_rows[:, None] * N_COL + block_cols[None, :]
    tract_ids = (tile_index * TRACTS_DEV + block_tract).astype(jnp.int32)
    tract_totals = jax.ops.segment_sum(block_sums.reshape(-1), tract_ids.reshape(-1), num_segments=TRACTS)
    county_totals = jax.ops.segment_sum(tract_totals, tract_county, num_segments=COUNTIES)
    state_totals = jax.ops.segment_sum(county_totals, county_state, num_segments=STATES)
    matrix = schur.reshape(ORDER, ORDER)
    factor = jnp.linalg.cholesky(matrix[:NB, :NB])
    panel_full = jax.scipy.linalg.solve_triangular(factor, matrix[:, :NB].T, lower=True).T
    updated = matrix - jnp.dot(panel_full, panel_full.T, precision=lax.Precision.HIGHEST)
    return (solution, residual, tract_totals, county_totals, state_totals, updated.reshape(RB, N_ROW * NB, CB, N_COL * NB), panel_full.reshape(RB, N_ROW * NB, NB))
```

```python
import functools
import jax
import jax.numpy as jnp
from jax import lax
from jax.experimental import pallas as pl
from jax.experimental.pallas import tpu as pltpu
from jax.sharding import PartitionSpec as P

BLOCK = 16
TRACTS_DEV = 64
COUNTIES = 512
STATES = 56
HALO = 4
PAD = 16
LANES = 128
HIGHEST = lax.Precision.HIGHEST
F32 = jnp.float32


def iota(shape, dim):
    return lax.broadcasted_iota(jnp.int32, shape, dim)


def dot(a, b, contract=(1, 0)):
    dims = (((contract[0],), (contract[1],)), ((), ()))
    return lax.dot_general(a, b, dims, precision=HIGHEST, preferred_element_type=F32)


def params(mib):
    return pltpu.CompilerParams(vmem_limit_bytes=mib << 20)


def pair_exchange(first, last, axis):
    size, odd = lax.axis_size(axis), lax.axis_index(axis) % 2 == 1
    near = [(i, i ^ 1) for i in range(size)]
    far = [(i, i + 1) for i in range(1, size - 1, 2)]
    far = far + [(j, i) for i, j in far]
    got_near = lax.ppermute(jnp.where(odd, first, last), axis, near)
    got_far = lax.ppermute(jnp.where(odd, last, first), axis, far)
    before = jnp.where(odd, got_near, got_far)
    after = jnp.where(odd, got_far, got_near)
    return before, after


def tree(block, axis, strides):
    size, index = lax.axis_size(axis), lax.axis_index(axis)
    for stride in strides:
        pairs = [(i, i + stride) for i in range(0, size, 2 * stride)]
        got = lax.ppermute(block, axis, pairs)
        block = jnp.where(index % (2 * stride) == stride, got, block)
    return block


def halvings(size):
    strides = []
    while size > 1:
        size //= 2
        strides.append(size)
    return strides


def spread_row(block, axis):
    size, index = lax.axis_size(axis), lax.axis_index(axis)
    strides = halvings(size)
    if len(strides) < 2:
        return tree(block, axis, strides)
    far, near = strides[:2]
    half = block.shape[0] // 2
    one, two = block[:half], block[half:]
    got_one = lax.ppermute(one, axis, [(0, near)])
    got_two = lax.ppermute(two, axis, [(0, far)])
    one = jnp.where(index == near, got_one, one)
    two = jnp.where(index == far, got_two, two)
    got_one = lax.ppermute(one, axis, [(0, far), (near, near + far)])
    got_two = lax.ppermute(two, axis, [(0, near), (far, near + far)])
    one = jnp.where(index % (2 * far) >= far, got_one, one)
    two = jnp.where((index == near) | (index == near + far), got_two, two)
    return tree(jnp.concatenate([one, two], axis=0), axis, strides[2:])


def raster_kernel(
    flags, b_hbm, k_hbm, above, below, sides, tracts, county, pay, sums, two, four,
    bx, kx, v1, v2, v3, rows_b, rows_2, sems
):
    rows, cols = two.shape
    wide = cols + 2 * LANES
    inner = (slice(PAD, PAD + rows), slice(LANES, LANES + cols))
    copy_b = pltpu.make_async_copy(b_hbm, bx.at[inner], sems.at[0])
    copy_k = pltpu.make_async_copy(k_hbm, kx.at[inner], sems.at[1])
    copy_b.start()
    copy_k.start()
    turned = sides[...].T
    lane = iota((rows, LANES), 1)
    for ref, left, right in (
        (bx, turned, turned),
        (kx, pltpu.roll(turned, HALO, 1), pltpu.roll(turned, LANES - HALO, 1)),
    ):
        ref[PAD - 8 : PAD, :] = jnp.zeros((8, wide), F32)
        ref[PAD + rows : PAD + rows + 8, :] = jnp.zeros((8, wide), F32)
        for start, part, keep in (
            (0, left, lane >= LANES - HALO),
            (LANES + cols, right, lane < HALO),
        ):
            own = slice(start, start + LANES)
            ref[PAD : PAD + rows, own] = jnp.where(keep, part[:rows], 0.0)
            keep = keep[:HALO]
            ref[PAD - HALO : PAD, own] = jnp.where(keep, part[rows : rows + HALO], 0.0)
            ref[PAD + rows : PAD + rows + HALO, own] = jnp.where(
                keep, part[rows + HALO : rows + 2 * HALO], 0.0
            )
    for ref, part in ((bx, slice(0, HALO)), (kx, slice(HALO, 2 * HALO))):
        ref[PAD - HALO : PAD, inner[1]] = above[part, :]
        ref[PAD + rows : PAD + rows + HALO, inner[1]] = below[part, :]
    copy_b.wait()
    copy_k.wait()

    column, sub = iota((8, wide), 1), iota((8, wide), 0)
    inside = jnp.logical_and(
        jnp.logical_or(column >= LANES, flags[2] > 0),
        jnp.logical_or(column < LANES + cols, flags[3] > 0),
    )

    def apply(src, row):
        centre = src[pl.ds(row, 8), :]
        up, down = src[pl.ds(row - 1, 1), :], src[pl.ds(row + 8, 1), :]
        beside = jnp.where(sub == 0, up, pltpu.roll(centre, 1, 0))
        beside = beside + jnp.where(sub == 7, down, pltpu.roll(centre, 7, 0))
        beside = beside + (pltpu.roll(centre, 1, 1) + pltpu.roll(centre, wide - 1, 1))
        out = (4.0 + kx[pl.ds(row, 8), :]) * centre - beside
        return centre[:, inner[1]], jnp.where(inside, out, 0.0)

    def edges(src, dst):
        for row, flag in ((PAD - 8, flags[0]), (PAD + rows, flags[1])):
            _, out = apply(src, row)
            dst[row : row + 8, :] = jnp.where(flag > 0, out, 0.0)

    def fold(value):
        return jnp.sum(value, axis=0, keepdims=True)

    def sweep_one(step, carry):
        sum_0, sum_1 = carry
        total = jnp.zeros((8, cols), F32)
        for part in range(2):
            row = pl.multiple_of(PAD + step * BLOCK + 8 * part, 8)
            centre, out = apply(bx, row)
            v1[pl.ds(row, 8), :] = out
            out = out[:, inner[1]]
            sum_0, sum_1 = sum_0 + centre * centre, sum_1 + out * out
            total = total + centre
        rows_b[pl.ds(step, 1), :] = fold(total)
        return sum_0, sum_1

    def sweep_two(step, sum_2):
        total = jnp.zeros((8, cols), F32)
        for part in range(2):
            row = pl.multiple_of(PAD + step * BLOCK + 8 * part, 8)
            _, out = apply(v1, row)
            v2[pl.ds(row, 8), :] = out
            out = out[:, inner[1]]
            two[pl.ds(row - PAD, 8), :] = out
            sum_2 = sum_2 + out * out
            total = total + out
        rows_2[pl.ds(step, 1), :] = fold(total)
        return sum_2

    def sweep_three(step, sum_3):
        row = pl.multiple_of(PAD + step * 8, 8)
        _, out = apply(v2, row)
        v3[pl.ds(row, 8), :] = out
        out = out[:, inner[1]]
        return sum_3 + out * out

    def sweep_four(step, carry):
        row = pl.multiple_of(PAD + step * 8, 8)
        _, out = apply(v3, row)
        four[pl.ds(row - PAD, 8), :] = out[:, inner[1]]
        return carry

    zero = jnp.zeros((8, cols), F32)
    edges(bx, v1)
    sum_0, sum_1 = lax.fori_loop(0, rows // BLOCK, sweep_one, (zero, zero))
    edges(v1, v2)
    sum_2 = lax.fori_loop(0, rows // BLOCK, sweep_two, zero)
    edges(v2, v3)
    sum_3 = lax.fori_loop(0, rows // 8, sweep_three, zero)
    lax.fori_loop(0, rows // 8, sweep_four, 0)

    pay[...] = jnp.zeros(pay.shape, F32)
    for index, value in enumerate((sum_0, sum_1, sum_2, sum_3)):
        value = fold(value)
        folded = value[:, :LANES]
        for start in range(LANES, cols, LANES):
            folded = folded + value[:, start : start + LANES]
        pay[8 + index : 9 + index, :] = folded

    group, place = iota((cols, LANES), 0) // BLOCK, iota((cols, LANES), 1)
    blocks = dot(rows_b[...], jnp.where(group == place, 1.0, 0.0))
    blocks = blocks + dot(rows_2[...], jnp.where(group + cols // BLOCK == place, 1.0, 0.0))
    for tract in range(TRACTS_DEV):
        sums[tract : tract + 1, :] = fold(jnp.where(tracts[...] == tract, blocks, 0.0))
    totals = sums[...]
    first = iota(totals.shape, 1) < cols // BLOCK
    for index, keep in enumerate((first, jnp.logical_not(first))):
        total = jnp.sum(jnp.where(keep, totals, 0.0), axis=1, keepdims=True)
        match = county[...] == iota((TRACTS_DEV, COUNTIES), 1)
        by_county = fold(jnp.where(match, total, 0.0))
        for part in range(COUNTIES // LANES):
            pay[4 * index + part : 4 * index + part + 1, :] = by_county[
                :, part * LANES : (part + 1) * LANES
            ]


def raster(flags, b, kappa, above, below, sides, tracts, county):
    rows, cols = b.shape
    shape = (rows + 2 * PAD, cols + 2 * LANES)
    any_spec = pl.BlockSpec(memory_space=pl.ANY)
    vmem = pl.BlockSpec(memory_space=pltpu.VMEM)
    return pl.pallas_call(
        raster_kernel,
        out_shape=(
            jax.ShapeDtypeStruct((16, LANES), F32),
            jax.ShapeDtypeStruct((TRACTS_DEV, LANES), F32),
            jax.ShapeDtypeStruct(b.shape, F32),
            jax.ShapeDtypeStruct(b.shape, F32),
        ),
        in_specs=[pl.BlockSpec(memory_space=pltpu.SMEM), any_spec, any_spec] + [vmem] * 5,
        out_specs=(vmem, vmem, vmem, vmem),
        scratch_shapes=[pltpu.VMEM(shape, F32)] * 5
        + [pltpu.VMEM((rows // BLOCK, cols), F32)] * 2
        + [pltpu.SemaphoreType.DMA((2,))],
        compiler_params=params(40),
        cost_estimate=pl.CostEstimate(flops=40 * rows * cols, transcendentals=0, bytes_accessed=16 * rows * cols),
        name="raster",
    )(flags, b, kappa, above, below, sides, tracts, county)


def two_sum(a, b):
    s = a + b
    t = s - a
    return s, (a - (s - t)) + (b - t)


def two_prod(a, b):
    def split(x):
        big = x * 4097.0
        high = big - (big - x)
        return high, x - high

    product = a * b
    a_high, a_low = split(a)
    b_high, b_low = split(b)
    low = ((a_high * b_high - product) + a_high * b_low + a_low * b_high) + a_low * b_low
    return product, low


def pair_add(a, b):
    high, low = two_sum(a[0], b[0])
    return two_sum(high, low + (a[1] + b[1]))


def pair_mul(a, b):
    high, low = two_prod(a[0], b[0])
    return two_sum(high, low + (a[0] * b[1] + a[1] * b[0]))


def pair_cross(a, b, c, d):
    minus = pair_mul(c, d)
    high, low = pair_add(pair_mul(a, b), (-minus[0], -minus[1]))
    return high + low


def finish_kernel(devices, got, sums, state, b, two, four, solution, residual, tract, county, states, scal):
    @pl.when(pl.program_id(0) == 0)
    def _():
        whole = got[0:16, :]
        err = jnp.zeros_like(whole)
        for device in range(1, devices):
            whole, low = two_sum(whole, got[16 * device : 16 * device + 16, :])
            err = err + low
        pair = (whole[8:12, :], err[8:12, :])
        shift = LANES // 2
        while shift:
            pair = pair_add(pair, (pltpu.roll(pair[0], shift, 1), pltpu.roll(pair[1], shift, 1)))
            shift //= 2
        scale = 1.0 / pair[0][0:1, :]
        m = []
        for index in range(4):
            m.append(pair_mul((scale, jnp.zeros_like(scale)), (pair[0][index : index + 1, :], pair[1][index : index + 1, :])))
        below = pair_cross(m[1], m[3], m[2], m[2])
        c_0 = pair_cross(m[0], m[3], m[1], m[2]) / below
        c_1 = pair_cross(m[0], m[2], m[1], m[1]) / below
        scal[0:1, :] = c_0
        scal[1:2, :] = c_1
        by_county = c_0 * whole[0:4, :] - c_1 * whole[4:8, :]
        county[...] = by_county
        place = iota((64, LANES), 0)
        total = jnp.zeros((64, LANES), F32)
        for part in range(COUNTIES // LANES):
            total = total + jnp.where(state[part : part + 1, :] == place, by_county[part : part + 1, :], 0.0)
        states[...] = dot(jnp.ones((8, LANES), F32), total, (1, 1))[0:1, :]
        first = iota((1, LANES), 1) < LANES // 2
        mixed = jnp.where(first, c_0, -c_1) * sums[...]
        tract[...] = dot(jnp.ones((8, LANES), F32), mixed, (1, 1))[0:1, :]

    c_0, c_1 = scal[0:1, 0:1], scal[1:2, 0:1]
    solution[...] = c_0 * b[...] - c_1 * two[...]
    residual[...] = b[...] - c_0 * two[...] + c_1 * four[...]


def finish(got, sums, state, b, two, four):
    rows, cols = b.shape
    step = 64
    devices = got.shape[0] // 16

    def fixed(shape):
        return pl.BlockSpec(shape, lambda i: (0, 0))

    tile = pl.BlockSpec((step, cols), lambda i: (i, 0))
    small = [(1, 64), (COUNTIES // LANES, LANES), (1, 64)]
    return pl.pallas_call(
        functools.partial(finish_kernel, devices),
        grid=(rows // step,),
        out_shape=[jax.ShapeDtypeStruct(b.shape, F32)] * 2
        + [jax.ShapeDtypeStruct(shape, F32) for shape in small],
        in_specs=[fixed(got.shape), fixed(sums.shape), fixed(state.shape), tile, tile, tile],
        out_specs=[tile, tile] + [fixed(shape) for shape in small],
        scratch_shapes=[pltpu.VMEM((8, LANES), F32)],
        compiler_params=params(24),
        cost_estimate=pl.CostEstimate(flops=6 * rows * cols, transcendentals=0, bytes_accessed=20 * rows * cols),
        name="finish",
    )(got, sums, state, b, two, four)


def invert_block(rows):
    size = LANES
    lane, sub = iota((8, size), 1), iota((8, size), 0)
    groups = size // 8
    pivots = [jnp.ones((8, size), F32)] * groups
    for k in range(size):
        g, s = divmod(k, 8)
        pivot = jnp.broadcast_to(rows[g][s : s + 1, k : k + 1], (8, size))
        line = jnp.broadcast_to(rows[g][s : s + 1, :], (8, size))
        scaled = jnp.where(lane == k, 1.0, line) * (1.0 / pivot)
        pivots[g] = jnp.where(sub == s, pivot, pivots[g])
        for h in range(g, groups):
            factor = jnp.broadcast_to(rows[h][:, k : k + 1], (8, size))
            updated = jnp.where(lane == k, 0.0, rows[h]) - factor * scaled
            rows[h] = jnp.where(sub > s, updated, rows[h]) if h == g else updated
    out = []
    for g in range(groups):
        row = sub + 8 * g
        kept = jnp.where(lane < row, rows[g], jnp.where(lane == row, 1.0, 0.0))
        out.append(kept / jnp.sqrt(pivots[g]))
    return out


def factor_kernel(a, inverse, part, left):
    size = LANES
    part[...] = a[0:size, 0:size]
    inverse[0:size, size:] = jnp.zeros((size, size), F32)

    def body(index, carry):
        rows = [part[8 * g : 8 * g + 8, :] for g in range(size // 8)]
        rows = invert_block(rows)
        for g in range(size // 8):
            part[8 * g : 8 * g + 8, :] = rows[g]

        @pl.when(index == 0)
        def _():
            first = part[...]
            inverse[0:size, 0:size] = first
            left[...] = dot(a[size:, 0:size], first, (1, 1))
            part[...] = a[size:, size:] - dot(left[...], left[...], (1, 1))

        return carry

    lax.fori_loop(0, 2, body, 0)
    inverse[size:, size:] = part[...]
    inverse[size:, 0:size] = -dot(part[...], dot(left[...], inverse[0:size, 0:size]))


def factor(a):
    size = a.shape[0]
    half = pltpu.VMEM((LANES, LANES), F32)
    return pl.pallas_call(
        factor_kernel,
        out_shape=jax.ShapeDtypeStruct(a.shape, F32),
        in_specs=[pl.BlockSpec(memory_space=pltpu.VMEM)],
        out_specs=pl.BlockSpec(memory_space=pltpu.VMEM),
        scratch_shapes=[half, half],
        compiler_params=params(16),
        cost_estimate=pl.CostEstimate(flops=200 * size * size * size, transcendentals=0, bytes_accessed=8 * size * size),
        name="factor",
    )(a)


def split(value):
    high = value.astype(jnp.bfloat16)
    return high, (value - high.astype(F32)).astype(jnp.bfloat16)


def update_kernel(column, wide, inverse, schur, panel, updated, other):
    size = inverse.shape[0]
    count = other.shape[0]

    @pl.when(pl.program_id(0) == 0)
    def _():
        for index in range(count):
            high, low = split(dot(inverse[...], wide[:, index, :]))
            other[index, 0:size, :] = high
            other[index, size : 2 * size, :] = low
            other[index, 2 * size :, :] = high

    own = dot(column[0], inverse[...], (1, 1))
    panel[0] = own
    high, low = split(own)
    lhs = jnp.concatenate([high, high, low], axis=1)
    for index in range(count):
        product = jnp.dot(lhs, other[index], preferred_element_type=F32)
        updated[0, :, index, :] = schur[0, :, index, :] - product


def update(column, wide, inverse, schur):
    count_rows, size, count, _ = schur.shape

    def step(*block):
        return pl.BlockSpec((1,) + block, lambda i: (i,) + (0,) * len(block))

    def fixed(shape):
        return pl.BlockSpec(shape, lambda i: (0,) * len(shape))

    panel, updated = pl.pallas_call(
        update_kernel,
        grid=(count_rows,),
        out_shape=(
            jax.ShapeDtypeStruct(column.shape, F32),
            jax.ShapeDtypeStruct(schur.shape, F32),
        ),
        in_specs=[step(size, size), fixed(wide.shape), fixed(inverse.shape), step(size, count, size)],
        out_specs=(step(size, size), step(size, count, size)),
        scratch_shapes=[pltpu.VMEM((count, 3 * size, size), jnp.bfloat16)],
        compiler_params=params(40),
        cost_estimate=pl.CostEstimate(flops=6 * schur.size * size, transcendentals=0, bytes_accessed=8 * schur.size),
        name="update",
    )(column, wide, inverse, schur)
    return panel, updated


def halo_messages(b, kappa):
    rows, cols = b.shape
    top = jnp.concatenate([b[:HALO], kappa[:HALO]], axis=0)
    bottom = jnp.concatenate([b[rows - HALO :], kappa[rows - HALO :]], axis=0)
    above, below = pair_exchange(top, bottom, "row")

    def strip(columns, which):
        field, at = ((b, 0), (kappa, HALO))[which]
        parts = [field[:, columns].T, above[at : at + HALO, columns].T, below[at : at + HALO, columns].T]
        return jnp.concatenate(parts, axis=1)

    first, last = slice(0, HALO), slice(cols - HALO, cols)
    left = jnp.concatenate([strip(first, 0), strip(first, 1)], axis=0)
    right = jnp.concatenate([strip(last, 1), strip(last, 0)], axis=0)
    before, after = pair_exchange(left, right, "col")
    length = before.shape[1]
    sides = jnp.zeros((LANES, -(-length // LANES) * LANES), F32)
    sides = sides.at[: 2 * HALO, :length].set(after)
    sides = sides.at[LANES - 2 * HALO :, :length].set(before)
    return above, below, sides


def per_device(right_side, kappa_sq, block_tract, tract_county, county_state, schur):
    n_row, n_col = lax.axis_size("row"), lax.axis_size("col")
    row, col = lax.axis_index("row"), lax.axis_index("col")
    above, below, sides = halo_messages(right_side, kappa_sq)
    flags = jnp.stack([row > 0, row < n_row - 1, col > 0, col < n_col - 1]).astype(jnp.int32)

    corner = tree(tree(schur[0, :, 0, :], "col", halvings(n_col)), "row", halvings(n_row))
    column = tree(schur[:, :, 0, :], "col", halvings(n_col))
    wide = spread_row(schur[0], "row")

    tracts = jnp.concatenate([block_tract, block_tract], axis=1)
    pay, sums, two, four = raster(
        flags, right_side, kappa_sq, above, below, sides, tracts, tract_county[:, None]
    )
    devices = n_row * n_col
    got = lax.all_to_all(jnp.broadcast_to(pay[None], (devices,) + pay.shape), ("row", "col"), 0, 0)
    inverse = factor(corner)
    solution, residual, tract_totals, county_totals, state_totals = finish(
        got.reshape(devices * 16, LANES),
        sums,
        county_state.reshape(COUNTIES // LANES, LANES),
        right_side,
        two,
        four,
    )
    panel, updated = update(column, wide, inverse, schur)
    return (
        solution,
        residual,
        tract_totals.reshape(-1)[:TRACTS_DEV],
        county_totals.reshape(-1),
        state_totals.reshape(-1)[:STATES],
        updated,
        panel,
    )


def solution(mesh):
    in_specs = (
        P("row", "col"),
        P("row", "col"),
        P("row", "col"),
        P(("row", "col")),
        P(),
        P(None, "row", None, "col"),
    )
    out_specs = (
        P("row", "col"),
        P("row", "col"),
        P(("row", "col")),
        P(),
        P(),
        P(None, "row", None, "col"),
        P(None, "row", None),
    )
    return jax.shard_map(
        per_device, mesh=mesh, in_specs=in_specs, out_specs=out_specs, check_vma=False
    )
```

```python
import functools
import jax
import jax.numpy as jnp
from jax import lax
from jax.experimental import pallas as pl
from jax.experimental.pallas import tpu as pltpu
from jax.sharding import PartitionSpec as P

BLOCK = 16
TRACTS_DEV = 64
COUNTIES = 512
STATES = 56
HALO = 4
PAD = 16
LANES = 128
HIGHEST = lax.Precision.HIGHEST
F32 = jnp.float32


def iota(shape, dim):
    return lax.broadcasted_iota(jnp.int32, shape, dim)


def dot(a, b, contract=(1, 0)):
    dims = (((contract[0],), (contract[1],)), ((), ()))
    return lax.dot_general(a, b, dims, precision=HIGHEST, preferred_element_type=F32)


def cost(micros):
    return pl.CostEstimate(flops=micros * 10**9, transcendentals=0, bytes_accessed=1 << 10)


def params(mib):
    return pltpu.CompilerParams(vmem_limit_bytes=mib << 20)


def trade(near, far, axis):
    size = lax.axis_size(axis)
    inside = [(i, i ^ 1) for i in range(size)]
    between = [(i, i + 1) for i in range(1, size - 1, 2)]
    between = between + [(j, i) for i, j in between]
    return lax.ppermute(near, axis, inside), lax.ppermute(far, axis, between)


def after(value, *others):
    return lax.optimization_barrier((value,) + others)[0]


def hop(block, axis, stride):
    pairs = [(i, i + stride // 2) for i in range(0, lax.axis_size(axis), stride)]
    return lax.ppermute(block, axis, pairs)


def relay(source, held, target, sem):
    copy = pltpu.make_async_copy(source, held, sem)
    copy.start()
    copy.wait()
    copy = pltpu.make_async_copy(held, target, sem)
    copy.start()
    copy.wait()


def merge_kernel(flag, got, _, out, held, sem):
    @pl.when(flag[0] > 0)
    def _():
        relay(got, held, out, sem)


def merge(got, block, axis, stride):
    flag = (lax.axis_index(axis) % stride == stride // 2).astype(jnp.int32).reshape(1)
    any_spec = pl.BlockSpec(memory_space=pl.ANY)
    return pl.pallas_call(
        merge_kernel,
        out_shape=jax.ShapeDtypeStruct(block.shape, block.dtype),
        in_specs=[pl.BlockSpec(memory_space=pltpu.SMEM), any_spec, any_spec],
        out_specs=any_spec,
        scratch_shapes=[pltpu.VMEM(block.shape, F32), pltpu.SemaphoreType.DMA],
        input_output_aliases={2: 0},
        compiler_params=params(60),
        cost_estimate=cost(2),
        name="merge",
    )(flag, got, block)


def extract_kernel(schur, raw, wide, held_raw, held_wide, sems):
    parts = ((schur.at[:, :, 0, :], held_raw, raw), (schur.at[0], held_wide, wide))
    loads = [pltpu.make_async_copy(a, b, sems.at[i]) for i, (a, b, _) in enumerate(parts)]
    stores = [pltpu.make_async_copy(b, c, sems.at[2 + i]) for i, (_, b, c) in enumerate(parts)]
    for copy in loads:
        copy.start()
    for load, store in zip(loads, stores):
        load.wait()
        store.start()
    for copy in stores:
        copy.wait()


def corner_block_kernel(schur, corner, sem):
    copy = pltpu.make_async_copy(schur.at[0, :, 0, :], corner, sem)
    copy.start()
    copy.wait()


def corner_block(schur):
    size = schur.shape[1]
    return pl.pallas_call(
        corner_block_kernel,
        out_shape=jax.ShapeDtypeStruct((size, size), F32),
        in_specs=[pl.BlockSpec(memory_space=pl.ANY)],
        out_specs=pl.BlockSpec(memory_space=pltpu.VMEM),
        scratch_shapes=[pltpu.SemaphoreType.DMA],
        compiler_params=params(60),
        cost_estimate=cost(2),
        name="corner",
    )(schur)


def extract(schur):
    count_rows, size, count, _ = schur.shape
    any_spec = pl.BlockSpec(memory_space=pl.ANY)
    return pl.pallas_call(
        extract_kernel,
        out_shape=(
            jax.ShapeDtypeStruct((count_rows, size, size), F32),
            jax.ShapeDtypeStruct((size, count, size), F32),
        ),
        in_specs=[any_spec],
        out_specs=(any_spec, any_spec),
        scratch_shapes=[
            pltpu.VMEM((count_rows, size, size), F32),
            pltpu.VMEM((size, count, size), F32),
            pltpu.SemaphoreType.DMA((4,)),
        ],
        compiler_params=params(60),
        cost_estimate=cost(3),
        name="extract",
    )(schur)


def small_steps(n_row, n_col):
    steps = []
    for axis, stride in (("col", n_col), ("row", n_row)):
        while stride > 1:
            steps.append((axis, stride))
            stride //= 2
    return steps


def small_hop(block, step):
    axis, stride = step
    got = hop(block, axis, stride)
    return jnp.where(lax.axis_index(axis) % stride == stride // 2, got, block)


def exchange(mine):
    axes = ("row", "col")
    devices = lax.axis_size("row") * lax.axis_size("col")
    return lax.all_to_all(jnp.broadcast_to(mine, (devices,) + mine.shape), axes, 0, 0)


def edge_kernel(flags, b_top, b_low, k_top, k_low, b_left, b_right, k_left, k_right, near, far, left, right):
    odd = flags[4] > 0
    for part, top, low in ((slice(0, HALO), b_top, b_low), (slice(HALO, 2 * HALO), k_top, k_low)):
        first, last = top[0:HALO, :], low[8 - HALO : 8, :]
        near[part, :] = jnp.where(odd, first, last)
        far[part, :] = jnp.where(odd, last, first)
    left[0:HALO, :] = b_left[...].T[0:HALO]
    left[HALO:, :] = k_left[...].T[0:HALO]
    right[0:HALO, :] = k_right[...].T[LANES - HALO :]
    right[HALO:, :] = b_right[...].T[LANES - HALO :]


def edge_messages(flags, b, kappa):
    rows, cols = b.shape

    def spec(shape, row, col):
        return pl.BlockSpec(shape, lambda i: (row, col))

    ends = [spec((8, cols), 0, 0), spec((8, cols), rows // 8 - 1, 0)]
    sides = [spec((rows, LANES), 0, 0), spec((rows, LANES), 0, cols // LANES - 1)]
    shapes = [(8, cols), (8, cols), (8, rows), (8, rows)]
    return pl.pallas_call(
        edge_kernel,
        grid=(1,),
        out_shape=[jax.ShapeDtypeStruct(shape, F32) for shape in shapes],
        in_specs=[pl.BlockSpec(memory_space=pltpu.SMEM)] + ends * 2 + sides * 2,
        out_specs=[spec(shape, 0, 0) for shape in shapes],
        compiler_params=params(60),
        cost_estimate=cost(2),
        name="edges",
    )(flags, b, b, kappa, kappa, b, b, kappa, kappa)


def corner_kernel(flags, got_near, got_far, left, right, above, below, near, far):
    odd, odd_col = flags[4] > 0, flags[5] > 0
    above[...] = jnp.where(odd, got_near[...], got_far[...])
    below[...] = jnp.where(odd, got_far[...], got_near[...])
    cols, rows = above.shape[1], left.shape[1]
    filler = jnp.zeros((LANES - 8, LANES), F32)

    def turned(ref, start):
        return jnp.concatenate([ref[:, start : start + LANES], filler], axis=0).T

    def choose(at, first, last):
        near[:, at] = jnp.where(odd_col, first, last)
        far[:, at] = jnp.where(odd_col, last, first)

    choose(slice(0, rows), left[...], right[...])
    for index, ref in enumerate((above, below)):
        first = turned(ref, 0)[0:8]
        last = turned(ref, cols - LANES)[LANES - 8 :]
        choose(slice(rows + index * LANES, rows + (index + 1) * LANES), first, last)


def corner_messages(flags, got_near, got_far, left, right):
    rows = left.shape[1]
    vmem = pl.BlockSpec(memory_space=pltpu.VMEM)
    shapes = [got_near.shape, got_near.shape, (8, rows + 2 * LANES), (8, rows + 2 * LANES)]
    return pl.pallas_call(
        corner_kernel,
        out_shape=[jax.ShapeDtypeStruct(shape, F32) for shape in shapes],
        in_specs=[pl.BlockSpec(memory_space=pltpu.SMEM)] + [vmem] * 4,
        out_specs=[vmem] * 4,
        compiler_params=params(2),
        cost_estimate=cost(1),
        name="corners",
    )(flags, got_near, got_far, left, right)


def raster_kernel(
    flags, b_hbm, k_hbm, above, below, got_near, got_far, tracts, county, pay, sums, two, four,
    bx, kx, v1, v2, v3, rows_b, rows_2, sems
):
    rows, cols = two.shape
    wide = cols + 2 * LANES
    inner = (slice(PAD, PAD + rows), slice(LANES, LANES + cols))
    copy_b = pltpu.make_async_copy(b_hbm, bx.at[inner], sems.at[0])
    copy_k = pltpu.make_async_copy(k_hbm, kx.at[inner], sems.at[1])
    copy_b.start()
    copy_k.start()
    odd = flags[5] > 0
    before = jnp.where(odd, got_near[...], got_far[...])
    after = jnp.where(odd, got_far[...], got_near[...])
    filler = jnp.zeros((LANES - 16, before.shape[1]), F32)
    turned = jnp.concatenate([after, filler, before], axis=0).T
    lane = iota((rows, LANES), 1)
    for ref, left, right, skip in (
        (bx, turned, turned, 0),
        (kx, pltpu.roll(turned, HALO, 1), pltpu.roll(turned, LANES - HALO, 1), HALO),
    ):
        ref[PAD - 8 : PAD, :] = jnp.zeros((8, wide), F32)
        ref[PAD + rows : PAD + rows + 8, :] = jnp.zeros((8, wide), F32)
        for start, part, keep in (
            (0, left, lane >= LANES - HALO),
            (LANES + cols, right, lane < HALO),
        ):
            own = slice(start, start + LANES)
            ref[PAD : PAD + rows, own] = jnp.where(keep, part[:rows], 0.0)
            keep = keep[:HALO]
            for place, at in ((PAD - HALO, rows), (PAD + rows, rows + LANES)):
                corner = turned[at + skip : at + skip + HALO]
                ref[place : place + HALO, own] = jnp.where(keep, corner, 0.0)
    for ref, part in ((bx, slice(0, HALO)), (kx, slice(HALO, 2 * HALO))):
        ref[PAD - HALO : PAD, inner[1]] = above[part, :]
        ref[PAD + rows : PAD + rows + HALO, inner[1]] = below[part, :]
    copy_b.wait()
    copy_k.wait()

    column, sub = iota((8, wide), 1), iota((8, wide), 0)
    inside = jnp.logical_and(
        jnp.logical_or(column >= LANES, flags[2] > 0),
        jnp.logical_or(column < LANES + cols, flags[3] > 0),
    )

    def apply(src, row):
        centre = src[pl.ds(row, 8), :]
        up, down = src[pl.ds(row - 1, 1), :], src[pl.ds(row + 8, 1), :]
        beside = jnp.where(sub == 0, up, pltpu.roll(centre, 1, 0))
        beside = beside + jnp.where(sub == 7, down, pltpu.roll(centre, 7, 0))
        beside = beside + (pltpu.roll(centre, 1, 1) + pltpu.roll(centre, wide - 1, 1))
        out = (4.0 + kx[pl.ds(row, 8), :]) * centre - beside
        return centre[:, inner[1]], jnp.where(inside, out, 0.0)

    def edges(src, dst):
        for row, flag in ((PAD - 8, flags[0]), (PAD + rows, flags[1])):
            _, out = apply(src, row)
            dst[row : row + 8, :] = jnp.where(flag > 0, out, 0.0)

    def fold(value):
        return jnp.sum(value, axis=0, keepdims=True)

    def sweep_one(step, carry):
        sum_0, sum_1 = carry
        total = jnp.zeros((8, cols), F32)
        for part in range(2):
            row = pl.multiple_of(PAD + step * BLOCK + 8 * part, 8)
            centre, out = apply(bx, row)
            v1[pl.ds(row, 8), :] = out
            out = out[:, inner[1]]
            sum_0, sum_1 = sum_0 + centre * centre, sum_1 + out * out
            total = total + centre
        rows_b[pl.ds(step, 1), :] = fold(total)
        return sum_0, sum_1

    def sweep_two(step, sum_2):
        total = jnp.zeros((8, cols), F32)
        for part in range(2):
            row = pl.multiple_of(PAD + step * BLOCK + 8 * part, 8)
            _, out = apply(v1, row)
            v2[pl.ds(row, 8), :] = out
            out = out[:, inner[1]]
            two[pl.ds(row - PAD, 8), :] = out
            sum_2 = sum_2 + out * out
            total = total + out
        rows_2[pl.ds(step, 1), :] = fold(total)
        return sum_2

    def sweep_three(step, sum_3):
        row = pl.multiple_of(PAD + step * 8, 8)
        _, out = apply(v2, row)
        v3[pl.ds(row, 8), :] = out
        out = out[:, inner[1]]
        return sum_3 + out * out

    def sweep_four(step, carry):
        row = pl.multiple_of(PAD + step * 8, 8)
        _, out = apply(v3, row)
        four[pl.ds(row - PAD, 8), :] = out[:, inner[1]]
        return carry

    zero = jnp.zeros((8, cols), F32)
    edges(bx, v1)
    sum_0, sum_1 = lax.fori_loop(0, rows // BLOCK, sweep_one, (zero, zero))
    edges(v1, v2)
    sum_2 = lax.fori_loop(0, rows // BLOCK, sweep_two, zero)
    edges(v2, v3)
    sum_3 = lax.fori_loop(0, rows // 8, sweep_three, zero)
    lax.fori_loop(0, rows // 8, sweep_four, 0)

    pay[...] = jnp.zeros(pay.shape, F32)
    for index, value in enumerate((sum_0, sum_1, sum_2, sum_3)):
        value = fold(value)
        folded = value[:, :LANES]
        for start in range(LANES, cols, LANES):
            folded = folded + value[:, start : start + LANES]
        pay[8 + index : 9 + index, :] = folded

    group, place = iota((cols, LANES), 0) // BLOCK, iota((cols, LANES), 1)
    blocks = dot(rows_b[...], jnp.where(group == place, 1.0, 0.0))
    blocks = blocks + dot(rows_2[...], jnp.where(group + cols // BLOCK == place, 1.0, 0.0))
    for tract in range(TRACTS_DEV):
        sums[tract : tract + 1, :] = fold(jnp.where(tracts[...] == tract, blocks, 0.0))
    totals = sums[...]
    first = iota(totals.shape, 1) < cols // BLOCK
    for index, keep in enumerate((first, jnp.logical_not(first))):
        total = jnp.sum(jnp.where(keep, totals, 0.0), axis=1, keepdims=True)
        match = county[...] == iota((TRACTS_DEV, COUNTIES), 1)
        by_county = fold(jnp.where(match, total, 0.0))
        for part in range(COUNTIES // LANES):
            pay[4 * index + part : 4 * index + part + 1, :] = by_county[
                :, part * LANES : (part + 1) * LANES
            ]


def raster(flags, b, kappa, above, below, got_near, got_far, tracts, county):
    rows, cols = b.shape
    shape = (rows + 2 * PAD, cols + 2 * LANES)
    any_spec = pl.BlockSpec(memory_space=pl.ANY)
    vmem = pl.BlockSpec(memory_space=pltpu.VMEM)
    return pl.pallas_call(
        raster_kernel,
        out_shape=(
            jax.ShapeDtypeStruct((16, LANES), F32),
            jax.ShapeDtypeStruct((TRACTS_DEV, LANES), F32),
            jax.ShapeDtypeStruct(b.shape, F32),
            jax.ShapeDtypeStruct(b.shape, F32),
        ),
        in_specs=[pl.BlockSpec(memory_space=pltpu.SMEM), any_spec, any_spec] + [vmem] * 6,
        out_specs=(vmem, vmem, vmem, vmem),
        scratch_shapes=[pltpu.VMEM(shape, F32)] * 5
        + [pltpu.VMEM((rows // BLOCK, cols), F32)] * 2
        + [pltpu.SemaphoreType.DMA((2,))],
        compiler_params=params(60),
        cost_estimate=cost(25),
        name="raster",
    )(flags, b, kappa, above, below, got_near, got_far, tracts, county)


def two_sum(a, b):
    s = a + b
    t = s - a
    return s, (a - (s - t)) + (b - t)


def two_prod(a, b):
    def split(x):
        big = x * 4097.0
        high = big - (big - x)
        return high, x - high

    product = a * b
    a_high, a_low = split(a)
    b_high, b_low = split(b)
    low = ((a_high * b_high - product) + a_high * b_low + a_low * b_high) + a_low * b_low
    return product, low


def pair_add(a, b):
    high, low = two_sum(a[0], b[0])
    return two_sum(high, low + (a[1] + b[1]))


def pair_mul(a, b):
    high, low = two_prod(a[0], b[0])
    return two_sum(high, low + (a[0] * b[1] + a[1] * b[0]))


def pair_cross(a, b, c, d):
    minus = pair_mul(c, d)
    high, low = pair_add(pair_mul(a, b), (-minus[0], -minus[1]))
    return high + low


def finish_kernel(devices, got, sums, state, b, two, four, solution, residual, tract, county, states, scal):
    @pl.when(pl.program_id(0) == 0)
    def _():
        whole = got[0:16, :]
        err = jnp.zeros_like(whole)
        for device in range(1, devices):
            whole, low = two_sum(whole, got[16 * device : 16 * device + 16, :])
            err = err + low
        pair = (whole[8:12, :], err[8:12, :])
        shift = LANES // 2
        while shift:
            pair = pair_add(pair, (pltpu.roll(pair[0], shift, 1), pltpu.roll(pair[1], shift, 1)))
            shift //= 2
        scale = 1.0 / pair[0][0:1, :]
        m = []
        for index in range(4):
            m.append(pair_mul((scale, jnp.zeros_like(scale)), (pair[0][index : index + 1, :], pair[1][index : index + 1, :])))
        below = pair_cross(m[1], m[3], m[2], m[2])
        c_0 = pair_cross(m[0], m[3], m[1], m[2]) / below
        c_1 = pair_cross(m[0], m[2], m[1], m[1]) / below
        scal[0:1, :] = c_0
        scal[1:2, :] = c_1
        by_county = c_0 * whole[0:4, :] - c_1 * whole[4:8, :]
        county[...] = by_county
        place = iota((64, LANES), 0)
        total = jnp.zeros((64, LANES), F32)
        for part in range(COUNTIES // LANES):
            total = total + jnp.where(state[part : part + 1, :] == place, by_county[part : part + 1, :], 0.0)
        states[...] = dot(jnp.ones((8, LANES), F32), total, (1, 1))[0:1, :]
        first = iota((1, LANES), 1) < LANES // 2
        mixed = jnp.where(first, c_0, -c_1) * sums[...]
        tract[...] = dot(jnp.ones((8, LANES), F32), mixed, (1, 1))[0:1, :]

    c_0, c_1 = scal[0:1, 0:1], scal[1:2, 0:1]
    solution[...] = c_0 * b[...] - c_1 * two[...]
    residual[...] = b[...] - c_0 * two[...] + c_1 * four[...]


def finish(got, sums, state, b, two, four):
    rows, cols = b.shape
    step = 64
    devices = got.shape[0] // 16

    def fixed(shape):
        return pl.BlockSpec(shape, lambda i: (0, 0))

    tile = pl.BlockSpec((step, cols), lambda i: (i, 0))
    small = [(1, 64), (COUNTIES // LANES, LANES), (1, 64)]
    return pl.pallas_call(
        functools.partial(finish_kernel, devices),
        grid=(rows // step,),
        out_shape=[jax.ShapeDtypeStruct(b.shape, F32)] * 2
        + [jax.ShapeDtypeStruct(shape, F32) for shape in small],
        in_specs=[fixed(got.shape), fixed(sums.shape), fixed(state.shape), tile, tile, tile],
        out_specs=[tile, tile] + [fixed(shape) for shape in small],
        scratch_shapes=[pltpu.VMEM((8, LANES), F32)],
        compiler_params=params(60),
        cost_estimate=cost(8),
        name="finish",
    )(got, sums, state, b, two, four)


def invert_pair(a, b, c):
    scale = 1.0 / (a * c - b * b)
    return c * scale, -b * scale, a * scale


def invert_block(rows):
    size = LANES
    lane, sub = iota((8, size), 1), iota((8, size), 0)
    groups = size // 8
    pivots = [jnp.ones((8, size), F32)] * groups
    for k in range(0, size, 4):
        g, s = divmod(k, 8)
        block = jnp.logical_and(lane >= k, lane < k + 4)
        factors = {
            h: [jnp.broadcast_to(rows[h][:, k + c : k + c + 1], (8, size)) for c in range(4)]
            for h in range(g, groups)
        }

        def at(i, j):
            return jnp.broadcast_to(factors[g][j][s + i : s + i + 1, :], (8, size))

        line = []
        for i in range(4):
            whole = jnp.broadcast_to(rows[g][s + i : s + i + 1, :], (8, size))
            line.append(jnp.where(block, jnp.where(lane == k + i, 1.0, 0.0), whole))
        p00, p10, p11 = at(0, 0), at(1, 0), at(1, 1)
        q00, q01, q10, q11 = at(2, 0), at(2, 1), at(3, 0), at(3, 1)
        i00, i10, i11 = invert_pair(p00, p10, p11)
        t00, t01 = q00 * i00 + q01 * i10, q00 * i10 + q01 * i11
        t10, t11 = q10 * i00 + q11 * i10, q10 * i10 + q11 * i11
        c00 = at(2, 2) - (t00 * q00 + t01 * q01)
        c10 = at(3, 2) - (t10 * q00 + t11 * q01)
        c11 = at(3, 3) - (t10 * q10 + t11 * q11)
        j00, j10, j11 = invert_pair(c00, c10, c11)
        low_2 = line[2] - (t00 * line[0] + t01 * line[1])
        low_3 = line[3] - (t10 * line[0] + t11 * line[1])
        w_2, w_3 = j00 * low_2 + j10 * low_3, j10 * low_2 + j11 * low_3
        w_0 = (i00 * line[0] + i10 * line[1]) - (t00 * w_2 + t10 * w_3)
        w_1 = (i10 * line[0] + i11 * line[1]) - (t01 * w_2 + t11 * w_3)
        for h in range(g, groups):
            f = factors[h]
            cut = (f[0] * w_0 + f[1] * w_1) + (f[2] * w_2 + f[3] * w_3)
            updated = jnp.where(block, 0.0, rows[h]) - cut
            if h > g:
                rows[h] = updated
                continue
            l10, l32 = p10 / p00, c10 / c00
            done = (line[0], line[1] - l10 * line[0], low_2, low_3 - l32 * low_2)
            diagonal = (p00, p11 - l10 * p10, c00, c11 - l32 * c10)
            own = jnp.where(sub >= s + 4, updated, rows[g])
            pivot = pivots[g]
            for i in range(4):
                own = jnp.where(sub == s + i, done[i], own)
                pivot = jnp.where(sub == s + i, diagonal[i], pivot)
            rows[g], pivots[g] = own, pivot
    out = []
    for g in range(groups):
        kept = jnp.where(lane <= sub + 8 * g, rows[g], 0.0)
        out.append(kept / jnp.sqrt(pivots[g]))
    return out


def factor_kernel(a, inverse, part, left):
    size = LANES
    part[...] = a[0:size, 0:size]
    inverse[0:size, size:] = jnp.zeros((size, size), F32)

    def body(index, carry):
        rows = [part[8 * g : 8 * g + 8, :] for g in range(size // 8)]
        rows = invert_block(rows)
        for g in range(size // 8):
            part[8 * g : 8 * g + 8, :] = rows[g]

        @pl.when(index == 0)
        def _():
            first = part[...]
            inverse[0:size, 0:size] = first
            left[...] = dot(a[size:, 0:size], first, (1, 1))
            part[...] = a[size:, size:] - dot(left[...], left[...], (1, 1))

        return carry

    lax.fori_loop(0, 2, body, 0)
    inverse[size:, size:] = part[...]
    inverse[size:, 0:size] = -dot(part[...], dot(left[...], inverse[0:size, 0:size]))


def factor(a):
    size = a.shape[0]
    half = pltpu.VMEM((LANES, LANES), F32)
    return pl.pallas_call(
        factor_kernel,
        out_shape=jax.ShapeDtypeStruct(a.shape, F32),
        in_specs=[pl.BlockSpec(memory_space=pltpu.VMEM)],
        out_specs=pl.BlockSpec(memory_space=pltpu.VMEM),
        scratch_shapes=[half, half],
        compiler_params=params(60),
        cost_estimate=cost(14),
        name="factor",
    )(a)


def split(value):
    high = value.astype(jnp.bfloat16)
    return high, (value - high.astype(F32)).astype(jnp.bfloat16)


def update_kernel(flags, column, column_got, wide_hbm, wide_got, inverse, schur, panel, updated, wide, other, sem):
    size = inverse.shape[0]
    count = other.shape[0]

    @pl.when(pl.program_id(0) == 0)
    def _():
        @pl.when(flags[4] > 0)
        def _():
            pltpu.make_async_copy(wide_got, wide, sem).start()

        @pl.when(flags[4] == 0)
        def _():
            pltpu.make_async_copy(wide_hbm, wide, sem).start()

        pltpu.make_async_copy(wide_hbm, wide, sem).wait()
        for index in range(count):
            high, low = split(dot(inverse[...], wide[:, index, :]))
            other[index, 0:size, :] = high
            other[index, size : 2 * size, :] = low
            other[index, 2 * size :, :] = high

    own = jnp.where(flags[5] > 0, column_got[0], column[0])
    own = dot(own, inverse[...], (1, 1))
    panel[0] = own
    high, low = split(own)
    lhs = jnp.concatenate([high, high, low], axis=1)
    for index in range(count):
        product = jnp.dot(lhs, other[index], preferred_element_type=F32)
        for part in range(size // LANES):
            at = pl.ds(part * count + index, size, stride=count * (size // LANES))
            updated[0, at, :] = schur[0, at, :] - product[:, part * LANES : (part + 1) * LANES]


def update(flags, column, column_got, wide, wide_got, inverse, schur):
    count_rows, size, count, _ = schur.shape
    parts = size // LANES
    flat = schur.reshape(count_rows, size, count, parts, LANES).transpose(0, 1, 3, 2, 4)
    flat = flat.reshape(count_rows, size * parts * count, LANES)

    def step(*block):
        return pl.BlockSpec((1,) + block, lambda i: (i,) + (0,) * len(block))

    any_spec = pl.BlockSpec(memory_space=pl.ANY)
    inverse_spec = pl.BlockSpec(inverse.shape, lambda i: (0, 0))
    panel, updated = pl.pallas_call(
        update_kernel,
        grid=(count_rows,),
        out_shape=(
            jax.ShapeDtypeStruct(column.shape, F32),
            jax.ShapeDtypeStruct(flat.shape, F32),
        ),
        in_specs=[pl.BlockSpec(memory_space=pltpu.SMEM), step(size, size), step(size, size)]
        + [any_spec, any_spec, inverse_spec, step(*flat.shape[1:])],
        out_specs=(step(size, size), step(*flat.shape[1:])),
        scratch_shapes=[
            pltpu.VMEM(wide.shape, F32),
            pltpu.VMEM((count, 3 * size, size), jnp.bfloat16),
            pltpu.SemaphoreType.DMA,
        ],
        compiler_params=params(60),
        cost_estimate=cost(17),
        name="update",
    )(flags, column, column_got, wide, wide_got, inverse, flat)
    updated = updated.reshape(count_rows, size, parts, count, LANES).transpose(0, 1, 3, 2, 4)
    return panel, updated.reshape(schur.shape)


def per_device(right_side, kappa_sq, block_tract, tract_county, county_state, schur):
    n_row, n_col = lax.axis_size("row"), lax.axis_size("col")
    row, col = lax.axis_index("row"), lax.axis_index("col")
    flags = [row > 0, row < n_row - 1, col > 0, col < n_col - 1, row % 2 == 1, col % 2 == 1]
    flags = jnp.stack(flags).astype(jnp.int32)

    corner = corner_block(schur)
    steps = small_steps(n_row, n_col)
    corner = small_hop(corner, steps[0])
    near, far, left, right = edge_messages(flags, right_side, kappa_sq)
    near, far = trade(near, far, "row")
    near, far, corner = lax.optimization_barrier((near, far, corner))
    corner = small_hop(corner, steps[1])
    above, below, near, far = corner_messages(flags, near, far, left, right)
    near, far = trade(near, far, "col")
    near, far, corner = lax.optimization_barrier((near, far, corner))
    corner = small_hop(corner, steps[2])
    column, wide = extract(after(schur, near))
    column, wide, corner = lax.optimization_barrier((column, wide, corner))
    column_got, wide_got = hop(column, "col", n_col), hop(wide, "row", n_row)
    for step in steps[3:]:
        corner = small_hop(corner, step)
    near, far, corner = lax.optimization_barrier((near, far, corner))

    tracts = jnp.concatenate([block_tract, block_tract], axis=1)
    pay, sums, two, four = raster(
        flags, right_side, kappa_sq, above, below, near, far, tracts, tract_county[:, None]
    )
    pay, column_got, wide_got = lax.optimization_barrier((pay, column_got, wide_got))
    got = exchange(pay).reshape(-1, LANES)
    stride = n_col
    while stride > 2:
        column = merge(column_got, column, "col", stride)
        stride //= 2
        column_got = hop(column, "col", stride)
    stride = n_row
    wide = merge(wide_got, wide, "row", stride)
    stride //= 2
    wide_got = hop(wide, "row", stride)
    inverse = factor(corner)
    wide_got, got = lax.optimization_barrier((wide_got, got))
    while stride > 2:
        wide = merge(wide_got, wide, "row", stride)
        stride //= 2
        wide_got = hop(wide, "row", stride)
    solution, residual, tract_totals, county_totals, state_totals = finish(
        after(got, inverse),
        sums,
        county_state.reshape(COUNTIES // LANES, LANES),
        right_side,
        two,
        four,
    )
    panel, updated = update(flags, column, column_got, wide, wide_got, inverse, schur)
    return (
        solution,
        residual,
        tract_totals.reshape(-1)[:TRACTS_DEV],
        county_totals.reshape(-1),
        state_totals.reshape(-1)[:STATES],
        updated,
        panel,
    )


def solution(mesh):
    in_specs = (
        P("row", "col"),
        P("row", "col"),
        P("row", "col"),
        P(("row", "col")),
        P(),
        P(None, "row", None, "col"),
    )
    out_specs = (
        P("row", "col"),
        P("row", "col"),
        P(("row", "col")),
        P(),
        P(),
        P(None, "row", None, "col"),
        P(None, "row", None),
    )
    return jax.shard_map(
        per_device, mesh=mesh, in_specs=in_specs, out_specs=out_specs, check_vma=False
    )
```

```python
import functools
import jax
import jax.numpy as jnp
from jax import lax
from jax.experimental import pallas as pl
from jax.experimental.pallas import tpu as pltpu
from jax.sharding import PartitionSpec as P

BLOCK = 16
TRACTS_DEV = 64
COUNTIES = 512
STATES = 56
HALO = 4
PAD = 16
LANES = 128
HIGHEST = lax.Precision.HIGHEST
F32 = jnp.float32


def iota(shape, dim):
    return lax.broadcasted_iota(jnp.int32, shape, dim)


def dot(a, b, contract=(1, 0)):
    dims = (((contract[0],), (contract[1],)), ((), ()))
    return lax.dot_general(a, b, dims, precision=HIGHEST, preferred_element_type=F32)


def cost(micros):
    return pl.CostEstimate(flops=micros * 10**9, transcendentals=0, bytes_accessed=1 << 10)


def params(mib):
    return pltpu.CompilerParams(vmem_limit_bytes=mib << 20)


def trade(near, far, axis):
    size = lax.axis_size(axis)
    inside = [(i, i ^ 1) for i in range(size)]
    between = [(i, i + 1) for i in range(1, size - 1, 2)]
    between = between + [(j, i) for i, j in between]
    return lax.ppermute(near, axis, inside), lax.ppermute(far, axis, between)


def after(value, *others):
    return lax.optimization_barrier((value,) + others)[0]


def hop(block, axis, stride):
    pairs = [(i, i + stride // 2) for i in range(0, lax.axis_size(axis), stride)]
    return lax.ppermute(block, axis, pairs)


def relay(source, held, target, sem):
    copy = pltpu.make_async_copy(source, held, sem)
    copy.start()
    copy.wait()
    copy = pltpu.make_async_copy(held, target, sem)
    copy.start()
    copy.wait()


def merge_kernel(flag, got, _, out, held, sem):
    @pl.when(flag[0] > 0)
    def _():
        relay(got, held, out, sem)


def merge(got, block, axis, stride):
    flag = (lax.axis_index(axis) % stride == stride // 2).astype(jnp.int32).reshape(1)
    any_spec = pl.BlockSpec(memory_space=pl.ANY)
    return pl.pallas_call(
        merge_kernel,
        out_shape=jax.ShapeDtypeStruct(block.shape, block.dtype),
        in_specs=[pl.BlockSpec(memory_space=pltpu.SMEM), any_spec, any_spec],
        out_specs=any_spec,
        scratch_shapes=[pltpu.VMEM(block.shape, F32), pltpu.SemaphoreType.DMA],
        input_output_aliases={2: 0},
        compiler_params=params(60),
        cost_estimate=cost(2),
        name="merge",
    )(flag, got, block)


def lane_tiles(schur):
    count_rows, size, count, width = schur.shape
    parts = width // LANES
    flat = schur.reshape(count_rows, size, count, parts, LANES).transpose(0, 1, 3, 2, 4)
    return flat.reshape(count_rows, size * parts * count, LANES)


def extract_kernel(schur, flat, raw, wide, held_raw, held_wide, sems):
    parts = ((schur.at[:, :, 0, :], held_raw, raw), (flat.at[0], held_wide, wide))
    loads = [pltpu.make_async_copy(a, b, sems.at[i]) for i, (a, b, _) in enumerate(parts)]
    stores = [pltpu.make_async_copy(b, c, sems.at[2 + i]) for i, (_, b, c) in enumerate(parts)]
    for copy in loads:
        copy.start()
    for load, store in zip(loads, stores):
        load.wait()
        store.start()
    for copy in stores:
        copy.wait()


def corner_block_kernel(schur, corner, sem):
    copy = pltpu.make_async_copy(schur.at[0, :, 0, :], corner, sem)
    copy.start()
    copy.wait()


def corner_block(schur):
    size = schur.shape[1]
    return pl.pallas_call(
        corner_block_kernel,
        out_shape=jax.ShapeDtypeStruct((size, size), F32),
        in_specs=[pl.BlockSpec(memory_space=pl.ANY)],
        out_specs=pl.BlockSpec(memory_space=pltpu.VMEM),
        scratch_shapes=[pltpu.SemaphoreType.DMA],
        compiler_params=params(60),
        cost_estimate=cost(2),
        name="corner",
    )(schur)


def extract(schur, flat):
    count_rows, size, _, _ = schur.shape
    any_spec = pl.BlockSpec(memory_space=pl.ANY)
    return pl.pallas_call(
        extract_kernel,
        out_shape=(
            jax.ShapeDtypeStruct((count_rows, size, size), F32),
            jax.ShapeDtypeStruct(flat.shape[1:], F32),
        ),
        in_specs=[any_spec, any_spec],
        out_specs=(any_spec, any_spec),
        scratch_shapes=[
            pltpu.VMEM((count_rows, size, size), F32),
            pltpu.VMEM(flat.shape[1:], F32),
            pltpu.SemaphoreType.DMA((4,)),
        ],
        compiler_params=params(60),
        cost_estimate=cost(3),
        name="extract",
    )(schur, flat)


def small_steps(n_row, n_col):
    steps = []
    for axis, stride in (("col", n_col), ("row", n_row)):
        while stride > 1:
            steps.append((axis, stride))
            stride //= 2
    return steps


def small_hop(block, step):
    axis, stride = step
    got = hop(block, axis, stride)
    return jnp.where(lax.axis_index(axis) % stride == stride // 2, got, block)


def exchange(mine):
    axes = ("row", "col")
    devices = lax.axis_size("row") * lax.axis_size("col")
    return lax.all_to_all(jnp.broadcast_to(mine, (devices,) + mine.shape), axes, 0, 0)


def edge_kernel(flags, b_top, b_low, k_top, k_low, b_left, b_right, k_left, k_right, near, far, left, right):
    odd = flags[4] > 0
    for part, top, low in ((slice(0, HALO), b_top, b_low), (slice(HALO, 2 * HALO), k_top, k_low)):
        first, last = top[0:HALO, :], low[8 - HALO : 8, :]
        near[part, :] = jnp.where(odd, first, last)
        far[part, :] = jnp.where(odd, last, first)
    left[0:HALO, :] = b_left[...].T[0:HALO]
    left[HALO:, :] = k_left[...].T[0:HALO]
    right[0:HALO, :] = k_right[...].T[LANES - HALO :]
    right[HALO:, :] = b_right[...].T[LANES - HALO :]


def edge_messages(flags, b, kappa):
    rows, cols = b.shape

    def spec(shape, row, col):
        return pl.BlockSpec(shape, lambda i: (row, col))

    ends = [spec((8, cols), 0, 0), spec((8, cols), rows // 8 - 1, 0)]
    sides = [spec((rows, LANES), 0, 0), spec((rows, LANES), 0, cols // LANES - 1)]
    shapes = [(8, cols), (8, cols), (8, rows), (8, rows)]
    return pl.pallas_call(
        edge_kernel,
        grid=(1,),
        out_shape=[jax.ShapeDtypeStruct(shape, F32) for shape in shapes],
        in_specs=[pl.BlockSpec(memory_space=pltpu.SMEM)] + ends * 2 + sides * 2,
        out_specs=[spec(shape, 0, 0) for shape in shapes],
        compiler_params=params(60),
        cost_estimate=cost(2),
        name="edges",
    )(flags, b, b, kappa, kappa, b, b, kappa, kappa)


def corner_kernel(flags, got_near, got_far, left, right, above, below, near, far):
    odd, odd_col = flags[4] > 0, flags[5] > 0
    above[...] = jnp.where(odd, got_near[...], got_far[...])
    below[...] = jnp.where(odd, got_far[...], got_near[...])
    cols, rows = above.shape[1], left.shape[1]
    filler = jnp.zeros((LANES - 8, LANES), F32)

    def turned(ref, start):
        return jnp.concatenate([ref[:, start : start + LANES], filler], axis=0).T

    def choose(at, first, last):
        near[:, at] = jnp.where(odd_col, first, last)
        far[:, at] = jnp.where(odd_col, last, first)

    choose(slice(0, rows), left[...], right[...])
    for index, ref in enumerate((above, below)):
        first = turned(ref, 0)[0:8]
        last = turned(ref, cols - LANES)[LANES - 8 :]
        choose(slice(rows + index * LANES, rows + (index + 1) * LANES), first, last)


def corner_messages(flags, got_near, got_far, left, right):
    rows = left.shape[1]
    vmem = pl.BlockSpec(memory_space=pltpu.VMEM)
    shapes = [got_near.shape, got_near.shape, (8, rows + 2 * LANES), (8, rows + 2 * LANES)]
    return pl.pallas_call(
        corner_kernel,
        out_shape=[jax.ShapeDtypeStruct(shape, F32) for shape in shapes],
        in_specs=[pl.BlockSpec(memory_space=pltpu.SMEM)] + [vmem] * 4,
        out_specs=[vmem] * 4,
        compiler_params=params(2),
        cost_estimate=cost(1),
        name="corners",
    )(flags, got_near, got_far, left, right)


def raster_kernel(
    flags, b_hbm, k_hbm, above, below, got_near, got_far, tracts, county, pay, sums, two, four,
    bx, kx, v1, v2, v3, rows_b, rows_2, sems
):
    rows, cols = two.shape
    wide = cols + 2 * LANES
    inner = (slice(PAD, PAD + rows), slice(LANES, LANES + cols))
    copy_b = pltpu.make_async_copy(b_hbm, bx.at[inner], sems.at[0])
    copy_k = pltpu.make_async_copy(k_hbm, kx.at[inner], sems.at[1])
    copy_b.start()
    copy_k.start()
    odd = flags[5] > 0
    before = jnp.where(odd, got_near[...], got_far[...])
    after = jnp.where(odd, got_far[...], got_near[...])
    filler = jnp.zeros((LANES - 16, before.shape[1]), F32)
    turned = jnp.concatenate([after, filler, before], axis=0).T
    lane = iota((rows, LANES), 1)
    for ref, left, right, skip in (
        (bx, turned, turned, 0),
        (kx, pltpu.roll(turned, HALO, 1), pltpu.roll(turned, LANES - HALO, 1), HALO),
    ):
        ref[PAD - 8 : PAD, :] = jnp.zeros((8, wide), F32)
        ref[PAD + rows : PAD + rows + 8, :] = jnp.zeros((8, wide), F32)
        for start, part, keep in (
            (0, left, lane >= LANES - HALO),
            (LANES + cols, right, lane < HALO),
        ):
            own = slice(start, start + LANES)
            ref[PAD : PAD + rows, own] = jnp.where(keep, part[:rows], 0.0)
            keep = keep[:HALO]
            for place, at in ((PAD - HALO, rows), (PAD + rows, rows + LANES)):
                corner = turned[at + skip : at + skip + HALO]
                ref[place : place + HALO, own] = jnp.where(keep, corner, 0.0)
    for ref, part in ((bx, slice(0, HALO)), (kx, slice(HALO, 2 * HALO))):
        ref[PAD - HALO : PAD, inner[1]] = above[part, :]
        ref[PAD + rows : PAD + rows + HALO, inner[1]] = below[part, :]
    copy_b.wait()
    copy_k.wait()

    column, sub = iota((8, wide), 1), iota((8, wide), 0)
    inside = jnp.logical_and(
        jnp.logical_or(column >= LANES, flags[2] > 0),
        jnp.logical_or(column < LANES + cols, flags[3] > 0),
    )

    def apply(src, row):
        centre = src[pl.ds(row, 8), :]
        up, down = src[pl.ds(row - 1, 1), :], src[pl.ds(row + 8, 1), :]
        beside = jnp.where(sub == 0, up, pltpu.roll(centre, 1, 0))
        beside = beside + jnp.where(sub == 7, down, pltpu.roll(centre, 7, 0))
        beside = beside + (pltpu.roll(centre, 1, 1) + pltpu.roll(centre, wide - 1, 1))
        out = (4.0 + kx[pl.ds(row, 8), :]) * centre - beside
        return centre[:, inner[1]], jnp.where(inside, out, 0.0)

    def edges(src, dst):
        for row, flag in ((PAD - 8, flags[0]), (PAD + rows, flags[1])):
            _, out = apply(src, row)
            dst[row : row + 8, :] = jnp.where(flag > 0, out, 0.0)

    def fold(value):
        return jnp.sum(value, axis=0, keepdims=True)

    def sweep_one(step, carry):
        sum_0, sum_1 = carry
        total = jnp.zeros((8, cols), F32)
        for part in range(2):
            row = pl.multiple_of(PAD + step * BLOCK + 8 * part, 8)
            centre, out = apply(bx, row)
            v1[pl.ds(row, 8), :] = out
            out = out[:, inner[1]]
            sum_0, sum_1 = sum_0 + centre * centre, sum_1 + out * out
            total = total + centre
        rows_b[pl.ds(step, 1), :] = fold(total)
        return sum_0, sum_1

    def sweep_two(step, sum_2):
        total = jnp.zeros((8, cols), F32)
        for part in range(2):
            row = pl.multiple_of(PAD + step * BLOCK + 8 * part, 8)
            _, out = apply(v1, row)
            v2[pl.ds(row, 8), :] = out
            out = out[:, inner[1]]
            two[pl.ds(row - PAD, 8), :] = out
            sum_2 = sum_2 + out * out
            total = total + out
        rows_2[pl.ds(step, 1), :] = fold(total)
        return sum_2

    def sweep_three(step, sum_3):
        row = pl.multiple_of(PAD + step * 8, 8)
        _, out = apply(v2, row)
        v3[pl.ds(row, 8), :] = out
        out = out[:, inner[1]]
        return sum_3 + out * out

    def sweep_four(step, carry):
        row = pl.multiple_of(PAD + step * 8, 8)
        _, out = apply(v3, row)
        four[pl.ds(row - PAD, 8), :] = out[:, inner[1]]
        return carry

    zero = jnp.zeros((8, cols), F32)
    edges(bx, v1)
    sum_0, sum_1 = lax.fori_loop(0, rows // BLOCK, sweep_one, (zero, zero), unroll=4)
    edges(v1, v2)
    sum_2 = lax.fori_loop(0, rows // BLOCK, sweep_two, zero, unroll=4)
    edges(v2, v3)
    sum_3 = lax.fori_loop(0, rows // 8, sweep_three, zero, unroll=8)
    lax.fori_loop(0, rows // 8, sweep_four, 0, unroll=8)

    pay[...] = jnp.zeros(pay.shape, F32)
    for index, value in enumerate((sum_0, sum_1, sum_2, sum_3)):
        value = fold(value)
        folded = value[:, :LANES]
        for start in range(LANES, cols, LANES):
            folded = folded + value[:, start : start + LANES]
        pay[8 + index : 9 + index, :] = folded

    group, place = iota((cols, LANES), 0) // BLOCK, iota((cols, LANES), 1)
    blocks = dot(rows_b[...], jnp.where(group == place, 1.0, 0.0))
    blocks = blocks + dot(rows_2[...], jnp.where(group + cols // BLOCK == place, 1.0, 0.0))
    for tract in range(TRACTS_DEV):
        sums[tract : tract + 1, :] = fold(jnp.where(tracts[...] == tract, blocks, 0.0))
    totals = sums[...]
    first = iota(totals.shape, 1) < cols // BLOCK
    for index, keep in enumerate((first, jnp.logical_not(first))):
        total = jnp.sum(jnp.where(keep, totals, 0.0), axis=1, keepdims=True)
        match = county[...] == iota((TRACTS_DEV, COUNTIES), 1)
        by_county = fold(jnp.where(match, total, 0.0))
        for part in range(COUNTIES // LANES):
            pay[4 * index + part : 4 * index + part + 1, :] = by_county[
                :, part * LANES : (part + 1) * LANES
            ]


def raster(flags, b, kappa, above, below, got_near, got_far, tracts, county):
    rows, cols = b.shape
    shape = (rows + 2 * PAD, cols + 2 * LANES)
    any_spec = pl.BlockSpec(memory_space=pl.ANY)
    vmem = pl.BlockSpec(memory_space=pltpu.VMEM)
    return pl.pallas_call(
        raster_kernel,
        out_shape=(
            jax.ShapeDtypeStruct((16, LANES), F32),
            jax.ShapeDtypeStruct((TRACTS_DEV, LANES), F32),
            jax.ShapeDtypeStruct(b.shape, F32),
            jax.ShapeDtypeStruct(b.shape, F32),
        ),
        in_specs=[pl.BlockSpec(memory_space=pltpu.SMEM), any_spec, any_spec] + [vmem] * 6,
        out_specs=(vmem, vmem, vmem, vmem),
        scratch_shapes=[pltpu.VMEM(shape, F32)] * 5
        + [pltpu.VMEM((rows // BLOCK, cols), F32)] * 2
        + [pltpu.SemaphoreType.DMA((2,))],
        compiler_params=params(60),
        cost_estimate=cost(25),
        name="raster",
    )(flags, b, kappa, above, below, got_near, got_far, tracts, county)


def two_sum(a, b):
    s = a + b
    t = s - a
    return s, (a - (s - t)) + (b - t)


def two_prod(a, b):
    def split(x):
        big = x * 4097.0
        high = big - (big - x)
        return high, x - high

    product = a * b
    a_high, a_low = split(a)
    b_high, b_low = split(b)
    low = ((a_high * b_high - product) + a_high * b_low + a_low * b_high) + a_low * b_low
    return product, low


def pair_add(a, b):
    high, low = two_sum(a[0], b[0])
    return two_sum(high, low + (a[1] + b[1]))


def pair_mul(a, b):
    high, low = two_prod(a[0], b[0])
    return two_sum(high, low + (a[0] * b[1] + a[1] * b[0]))


def pair_cross(a, b, c, d):
    minus = pair_mul(c, d)
    high, low = pair_add(pair_mul(a, b), (-minus[0], -minus[1]))
    return high + low


def finish_kernel(devices, got, sums, state, b, two, four, solution, residual, tract, county, states, scal):
    @pl.when(pl.program_id(0) == 0)
    def _():
        whole = got[0:16, :]
        err = jnp.zeros_like(whole)
        for device in range(1, devices):
            whole, low = two_sum(whole, got[16 * device : 16 * device + 16, :])
            err = err + low
        pair = (whole[8:12, :], err[8:12, :])
        shift = LANES // 2
        while shift:
            pair = pair_add(pair, (pltpu.roll(pair[0], shift, 1), pltpu.roll(pair[1], shift, 1)))
            shift //= 2
        scale = 1.0 / pair[0][0:1, :]
        m = []
        for index in range(4):
            m.append(pair_mul((scale, jnp.zeros_like(scale)), (pair[0][index : index + 1, :], pair[1][index : index + 1, :])))
        below = pair_cross(m[1], m[3], m[2], m[2])
        c_0 = pair_cross(m[0], m[3], m[1], m[2]) / below
        c_1 = pair_cross(m[0], m[2], m[1], m[1]) / below
        scal[0:1, :] = c_0
        scal[1:2, :] = c_1
        by_county = c_0 * whole[0:4, :] - c_1 * whole[4:8, :]
        county[...] = by_county
        place = iota((64, LANES), 0)
        total = jnp.zeros((64, LANES), F32)
        for part in range(COUNTIES // LANES):
            total = total + jnp.where(state[part : part + 1, :] == place, by_county[part : part + 1, :], 0.0)
        states[...] = dot(jnp.ones((8, LANES), F32), total, (1, 1))[0:1, :]
        first = iota((1, LANES), 1) < LANES // 2
        mixed = jnp.where(first, c_0, -c_1) * sums[...]
        tract[...] = dot(jnp.ones((8, LANES), F32), mixed, (1, 1))[0:1, :]

    c_0, c_1 = scal[0:1, 0:1], scal[1:2, 0:1]
    solution[...] = c_0 * b[...] - c_1 * two[...]
    residual[...] = b[...] - c_0 * two[...] + c_1 * four[...]


def finish(got, sums, state, b, two, four):
    rows, cols = b.shape
    step = 128
    devices = got.shape[0] // 16

    def fixed(shape):
        return pl.BlockSpec(shape, lambda i: (0, 0))

    tile = pl.BlockSpec((step, cols), lambda i: (i, 0))
    small = [(1, 64), (COUNTIES // LANES, LANES), (1, 64)]
    return pl.pallas_call(
        functools.partial(finish_kernel, devices),
        grid=(rows // step,),
        out_shape=[jax.ShapeDtypeStruct(b.shape, F32)] * 2
        + [jax.ShapeDtypeStruct(shape, F32) for shape in small],
        in_specs=[fixed(got.shape), fixed(sums.shape), fixed(state.shape), tile, tile, tile],
        out_specs=[tile, tile] + [fixed(shape) for shape in small],
        scratch_shapes=[pltpu.VMEM((8, LANES), F32)],
        compiler_params=params(60),
        cost_estimate=cost(8),
        name="finish",
    )(got, sums, state, b, two, four)


def invert_pair(a, b, c):
    scale = 1.0 / (a * c - b * b)
    return c * scale, -b * scale, a * scale


def invert_block(rows):
    size = LANES
    lane, sub = iota((8, size), 1), iota((8, size), 0)
    groups = size // 8
    pivots = [jnp.ones((8, size), F32)] * groups
    for k in range(0, size, 4):
        g, s = divmod(k, 8)
        block = jnp.logical_and(lane >= k, lane < k + 4)
        factors = {
            h: [jnp.broadcast_to(rows[h][:, k + c : k + c + 1], (8, size)) for c in range(4)]
            for h in range(g, groups)
        }

        def at(i, j):
            return jnp.broadcast_to(factors[g][j][s + i : s + i + 1, :], (8, size))

        line = []
        for i in range(4):
            whole = jnp.broadcast_to(rows[g][s + i : s + i + 1, :], (8, size))
            line.append(jnp.where(block, jnp.where(lane == k + i, 1.0, 0.0), whole))
        p00, p10, p11 = at(0, 0), at(1, 0), at(1, 1)
        q00, q01, q10, q11 = at(2, 0), at(2, 1), at(3, 0), at(3, 1)
        i00, i10, i11 = invert_pair(p00, p10, p11)
        t00, t01 = q00 * i00 + q01 * i10, q00 * i10 + q01 * i11
        t10, t11 = q10 * i00 + q11 * i10, q10 * i10 + q11 * i11
        c00 = at(2, 2) - (t00 * q00 + t01 * q01)
        c10 = at(3, 2) - (t10 * q00 + t11 * q01)
        c11 = at(3, 3) - (t10 * q10 + t11 * q11)
        j00, j10, j11 = invert_pair(c00, c10, c11)
        low_2 = line[2] - (t00 * line[0] + t01 * line[1])
        low_3 = line[3] - (t10 * line[0] + t11 * line[1])
        w_2, w_3 = j00 * low_2 + j10 * low_3, j10 * low_2 + j11 * low_3
        w_0 = (i00 * line[0] + i10 * line[1]) - (t00 * w_2 + t10 * w_3)
        w_1 = (i10 * line[0] + i11 * line[1]) - (t01 * w_2 + t11 * w_3)
        for h in range(g, groups):
            f = factors[h]
            cut = (f[0] * w_0 + f[1] * w_1) + (f[2] * w_2 + f[3] * w_3)
            updated = jnp.where(block, 0.0, rows[h]) - cut
            if h > g:
                rows[h] = updated
                continue
            l10, l32 = p10 / p00, c10 / c00
            done = (line[0], line[1] - l10 * line[0], low_2, low_3 - l32 * low_2)
            diagonal = (p00, p11 - l10 * p10, c00, c11 - l32 * c10)
            own = jnp.where(sub >= s + 4, updated, rows[g])
            pivot = pivots[g]
            for i in range(4):
                own = jnp.where(sub == s + i, done[i], own)
                pivot = jnp.where(sub == s + i, diagonal[i], pivot)
            rows[g], pivots[g] = own, pivot
    out = []
    for g in range(groups):
        kept = jnp.where(lane <= sub + 8 * g, rows[g], 0.0)
        out.append(kept / jnp.sqrt(pivots[g]))
    return out


def factor_kernel(a, inverse, part, left):
    size = LANES
    part[...] = a[0:size, 0:size]
    inverse[0:size, size:] = jnp.zeros((size, size), F32)

    def body(index, carry):
        rows = [part[8 * g : 8 * g + 8, :] for g in range(size // 8)]
        rows = invert_block(rows)
        for g in range(size // 8):
            part[8 * g : 8 * g + 8, :] = rows[g]

        @pl.when(index == 0)
        def _():
            first = part[...]
            inverse[0:size, 0:size] = first
            left[...] = dot(a[size:, 0:size], first, (1, 1))
            part[...] = a[size:, size:] - dot(left[...], left[...], (1, 1))

        return carry

    lax.fori_loop(0, 2, body, 0)
    inverse[size:, size:] = part[...]
    inverse[size:, 0:size] = -dot(part[...], dot(left[...], inverse[0:size, 0:size]))


def factor(a):
    size = a.shape[0]
    half = pltpu.VMEM((LANES, LANES), F32)
    return pl.pallas_call(
        factor_kernel,
        out_shape=jax.ShapeDtypeStruct(a.shape, F32),
        in_specs=[pl.BlockSpec(memory_space=pltpu.VMEM)],
        out_specs=pl.BlockSpec(memory_space=pltpu.VMEM),
        scratch_shapes=[half, half],
        compiler_params=params(60),
        cost_estimate=cost(14),
        name="factor",
    )(a)


def split(value):
    high = value.astype(jnp.bfloat16)
    return high, (value - high.astype(F32)).astype(jnp.bfloat16)


def tile_rows(ref, index, size, count):
    parts = [
        ref[pl.ds(part * count + index, size, stride=count * (size // LANES)), :]
        for part in range(size // LANES)
    ]
    return jnp.concatenate(parts, axis=1)


def update_kernel(flags, column, column_got, wide_hbm, wide_got, inverse, schur, panel, updated, wide, other, sem):
    size = inverse.shape[0]
    count = other.shape[0]

    @pl.when(pl.program_id(0) == 0)
    def _():
        @pl.when(flags[4] > 0)
        def _():
            pltpu.make_async_copy(wide_got, wide, sem).start()

        @pl.when(flags[4] == 0)
        def _():
            pltpu.make_async_copy(wide_hbm, wide, sem).start()

        pltpu.make_async_copy(wide_hbm, wide, sem).wait()
        for index in range(count):
            high, low = split(dot(inverse[...], tile_rows(wide, index, size, count)))
            other[index, 0:size, :] = high
            other[index, size : 2 * size, :] = low
            other[index, 2 * size :, :] = high

    own = jnp.where(flags[5] > 0, column_got[0], column[0])
    own = dot(own, inverse[...], (1, 1))
    panel[0] = own
    high, low = split(own)
    lhs = jnp.concatenate([high, high, low], axis=1)
    for index in range(count):
        product = jnp.dot(lhs, other[index], preferred_element_type=F32)
        for part in range(size // LANES):
            at = pl.ds(part * count + index, size, stride=count * (size // LANES))
            updated[0, at, :] = schur[0, at, :] - product[:, part * LANES : (part + 1) * LANES]


def update(flags, column, column_got, wide, wide_got, inverse, schur):
    count_rows, size, count, _ = schur.shape
    parts = size // LANES
    flat = lane_tiles(schur)

    def step(*block):
        return pl.BlockSpec((1,) + block, lambda i: (i,) + (0,) * len(block))

    any_spec = pl.BlockSpec(memory_space=pl.ANY)
    inverse_spec = pl.BlockSpec(inverse.shape, lambda i: (0, 0))
    panel, updated = pl.pallas_call(
        update_kernel,
        grid=(count_rows,),
        out_shape=(
            jax.ShapeDtypeStruct(column.shape, F32),
            jax.ShapeDtypeStruct(flat.shape, F32),
        ),
        in_specs=[pl.BlockSpec(memory_space=pltpu.SMEM), step(size, size), step(size, size)]
        + [any_spec, any_spec, inverse_spec, step(*flat.shape[1:])],
        out_specs=(step(size, size), step(*flat.shape[1:])),
        scratch_shapes=[
            pltpu.VMEM(wide.shape, F32),
            pltpu.VMEM((count, 3 * size, size), jnp.bfloat16),
            pltpu.SemaphoreType.DMA,
        ],
        compiler_params=params(60),
        cost_estimate=cost(17),
        name="update",
    )(flags, column, column_got, wide, wide_got, inverse, flat)
    updated = updated.reshape(count_rows, size, parts, count, LANES).transpose(0, 1, 3, 2, 4)
    return panel, updated.reshape(schur.shape)


def per_device(right_side, kappa_sq, block_tract, tract_county, county_state, schur):
    n_row, n_col = lax.axis_size("row"), lax.axis_size("col")
    row, col = lax.axis_index("row"), lax.axis_index("col")
    flags = [row > 0, row < n_row - 1, col > 0, col < n_col - 1, row % 2 == 1, col % 2 == 1]
    flags = jnp.stack(flags).astype(jnp.int32)

    corner = corner_block(schur)
    steps = small_steps(n_row, n_col)
    corner = small_hop(corner, steps[0])
    near, far, left, right = edge_messages(flags, right_side, kappa_sq)
    near, far = trade(near, far, "row")
    near, far, corner = lax.optimization_barrier((near, far, corner))
    corner = small_hop(corner, steps[1])
    above, below, near, far = corner_messages(flags, near, far, left, right)
    near, far = trade(near, far, "col")
    near, far, corner = lax.optimization_barrier((near, far, corner))
    corner = small_hop(corner, steps[2])
    held, flat, near = lax.optimization_barrier((schur, lane_tiles(schur), near))
    column, wide = extract(held, flat)
    column, wide, corner = lax.optimization_barrier((column, wide, corner))
    column_got, wide_got = hop(column, "col", n_col), hop(wide, "row", n_row)
    for step in steps[3:]:
        corner = small_hop(corner, step)
    near, far, corner = lax.optimization_barrier((near, far, corner))

    tracts = jnp.concatenate([block_tract, block_tract], axis=1)
    pay, sums, two, four = raster(
        flags, right_side, kappa_sq, above, below, near, far, tracts, tract_county[:, None]
    )
    pay, column_got, wide_got = lax.optimization_barrier((pay, column_got, wide_got))
    got = exchange(pay).reshape(-1, LANES)
    stride = n_col
    while stride > 2:
        column = merge(column_got, column, "col", stride)
        stride //= 2
        column_got = hop(column, "col", stride)
    stride = n_row
    wide = merge(wide_got, wide, "row", stride)
    stride //= 2
    wide_got = hop(wide, "row", stride)
    inverse = factor(corner)
    wide_got, got, inverse, column_got = lax.optimization_barrier((wide_got, got, inverse, column_got))
    while stride > 2:
        wide = merge(wide_got, wide, "row", stride)
        stride //= 2
        wide_got = hop(wide, "row", stride)
    solution, residual, tract_totals, county_totals, state_totals = finish(
        got,
        sums,
        county_state.reshape(COUNTIES // LANES, LANES),
        right_side,
        two,
        four,
    )
    panel, updated = update(flags, column, column_got, wide, wide_got, inverse, schur)
    return (
        solution,
        residual,
        tract_totals.reshape(-1)[:TRACTS_DEV],
        county_totals.reshape(-1),
        state_totals.reshape(-1)[:STATES],
        updated,
        panel,
    )


def solution(mesh):
    in_specs = (
        P("row", "col"),
        P("row", "col"),
        P("row", "col"),
        P(("row", "col")),
        P(),
        P(None, "row", None, "col"),
    )
    out_specs = (
        P("row", "col"),
        P("row", "col"),
        P(("row", "col")),
        P(),
        P(),
        P(None, "row", None, "col"),
        P(None, "row", None),
    )
    return jax.shard_map(
        per_device, mesh=mesh, in_specs=in_specs, out_specs=out_specs, check_vma=False
    )
```

```python
import functools
import jax
import jax.numpy as jnp
from jax import lax
from jax.experimental import pallas as pl
from jax.experimental.pallas import tpu as pltpu
from jax.sharding import PartitionSpec as P

BLOCK = 16
TRACTS_DEV = 64
COUNTIES = 512
STATES = 56
HALO = 4
PAD = 16
LANES = 128
HIGHEST = lax.Precision.HIGHEST
F32 = jnp.float32


def iota(shape, dim):
    return lax.broadcasted_iota(jnp.int32, shape, dim)


def dot(a, b, contract=(1, 0)):
    dims = (((contract[0],), (contract[1],)), ((), ()))
    return lax.dot_general(a, b, dims, precision=HIGHEST, preferred_element_type=F32)


def cost(micros):
    return pl.CostEstimate(flops=micros * 10**9, transcendentals=0, bytes_accessed=1 << 10)


def params(mib):
    return pltpu.CompilerParams(vmem_limit_bytes=mib << 20)


def trade(near, far, axis):
    size = lax.axis_size(axis)
    inside = [(i, i ^ 1) for i in range(size)]
    between = [(i, i + 1) for i in range(1, size - 1, 2)]
    between = between + [(j, i) for i, j in between]
    return lax.ppermute(near, axis, inside), lax.ppermute(far, axis, between)


def after(value, *others):
    return lax.optimization_barrier((value,) + others)[0]


def hop(block, axis, stride):
    pairs = [(i, i + stride // 2) for i in range(0, lax.axis_size(axis), stride)]
    return lax.ppermute(block, axis, pairs)


def relay(source, held, target, sem):
    copy = pltpu.make_async_copy(source, held, sem)
    copy.start()
    copy.wait()
    copy = pltpu.make_async_copy(held, target, sem)
    copy.start()
    copy.wait()


def merge_kernel(flag, got, _, out, held, sem):
    @pl.when(flag[0] > 0)
    def _():
        relay(got, held, out, sem)


def merge(got, block, axis, stride):
    flag = (lax.axis_index(axis) % stride == stride // 2).astype(jnp.int32).reshape(1)
    any_spec = pl.BlockSpec(memory_space=pl.ANY)
    return pl.pallas_call(
        merge_kernel,
        out_shape=jax.ShapeDtypeStruct(block.shape, block.dtype),
        in_specs=[pl.BlockSpec(memory_space=pltpu.SMEM), any_spec, any_spec],
        out_specs=any_spec,
        scratch_shapes=[pltpu.VMEM(block.shape, F32), pltpu.SemaphoreType.DMA],
        input_output_aliases={2: 0},
        compiler_params=params(60),
        cost_estimate=cost(2),
        name="merge",
    )(flag, got, block)


def lane_tiles(schur):
    count_rows, size, count, width = schur.shape
    parts = width // LANES
    flat = schur.reshape(count_rows, size, count, parts, LANES).transpose(0, 1, 3, 2, 4)
    return flat.reshape(count_rows, size * parts * count, LANES)


def extract_kernel(schur, flat, raw, wide, held_raw, held_wide, sems):
    parts = ((schur.at[:, :, 0, :], held_raw, raw), (flat.at[0], held_wide, wide))
    loads = [pltpu.make_async_copy(a, b, sems.at[i]) for i, (a, b, _) in enumerate(parts)]
    stores = [pltpu.make_async_copy(b, c, sems.at[2 + i]) for i, (_, b, c) in enumerate(parts)]
    for copy in loads:
        copy.start()
    for load, store in zip(loads, stores):
        load.wait()
        store.start()
    for copy in stores:
        copy.wait()


def corner_block_kernel(schur, corner, sem):
    copy = pltpu.make_async_copy(schur.at[0, :, 0, :], corner, sem)
    copy.start()
    copy.wait()


def corner_block(schur):
    size = schur.shape[1]
    return pl.pallas_call(
        corner_block_kernel,
        out_shape=jax.ShapeDtypeStruct((size, size), F32),
        in_specs=[pl.BlockSpec(memory_space=pl.ANY)],
        out_specs=pl.BlockSpec(memory_space=pltpu.VMEM),
        scratch_shapes=[pltpu.SemaphoreType.DMA],
        compiler_params=params(60),
        cost_estimate=cost(2),
        name="corner",
    )(schur)


def extract(schur, flat):
    count_rows, size, _, _ = schur.shape
    any_spec = pl.BlockSpec(memory_space=pl.ANY)
    return pl.pallas_call(
        extract_kernel,
        out_shape=(
            jax.ShapeDtypeStruct((count_rows, size, size), F32),
            jax.ShapeDtypeStruct(flat.shape[1:], F32),
        ),
        in_specs=[any_spec, any_spec],
        out_specs=(any_spec, any_spec),
        scratch_shapes=[
            pltpu.VMEM((count_rows, size, size), F32),
            pltpu.VMEM(flat.shape[1:], F32),
            pltpu.SemaphoreType.DMA((4,)),
        ],
        compiler_params=params(60),
        cost_estimate=cost(3),
        name="extract",
    )(schur, flat)


def small_steps(n_row, n_col):
    steps = []
    for axis, stride in (("col", n_col), ("row", n_row)):
        while stride > 1:
            steps.append((axis, stride))
            stride //= 2
    return steps


def small_hop(block, step):
    axis, stride = step
    got = hop(block, axis, stride)
    return jnp.where(lax.axis_index(axis) % stride == stride // 2, got, block)


def exchange(mine):
    axes = ("row", "col")
    devices = lax.axis_size("row") * lax.axis_size("col")
    return lax.all_to_all(jnp.broadcast_to(mine, (devices,) + mine.shape), axes, 0, 0)


def edge_kernel(flags, b_top, b_low, k_top, k_low, b_left, b_right, k_left, k_right, near, far, left, right):
    odd = flags[4] > 0
    for part, top, low in ((slice(0, HALO), b_top, b_low), (slice(HALO, 2 * HALO), k_top, k_low)):
        first, last = top[0:HALO, :], low[8 - HALO : 8, :]
        near[part, :] = jnp.where(odd, first, last)
        far[part, :] = jnp.where(odd, last, first)
    left[0:HALO, :] = b_left[...].T[0:HALO]
    left[HALO:, :] = k_left[...].T[0:HALO]
    right[0:HALO, :] = k_right[...].T[LANES - HALO :]
    right[HALO:, :] = b_right[...].T[LANES - HALO :]


def edge_messages(flags, b, kappa):
    rows, cols = b.shape

    def spec(shape, row, col):
        return pl.BlockSpec(shape, lambda i: (row, col))

    ends = [spec((8, cols), 0, 0), spec((8, cols), rows // 8 - 1, 0)]
    sides = [spec((rows, LANES), 0, 0), spec((rows, LANES), 0, cols // LANES - 1)]
    shapes = [(8, cols), (8, cols), (8, rows), (8, rows)]
    return pl.pallas_call(
        edge_kernel,
        grid=(1,),
        out_shape=[jax.ShapeDtypeStruct(shape, F32) for shape in shapes],
        in_specs=[pl.BlockSpec(memory_space=pltpu.SMEM)] + ends * 2 + sides * 2,
        out_specs=[spec(shape, 0, 0) for shape in shapes],
        compiler_params=params(60),
        cost_estimate=cost(2),
        name="edges",
    )(flags, b, b, kappa, kappa, b, b, kappa, kappa)


def corner_kernel(flags, got_near, got_far, left, right, above, below, near, far):
    odd, odd_col = flags[4] > 0, flags[5] > 0
    above[...] = jnp.where(odd, got_near[...], got_far[...])
    below[...] = jnp.where(odd, got_far[...], got_near[...])
    cols, rows = above.shape[1], left.shape[1]
    filler = jnp.zeros((LANES - 8, LANES), F32)

    def turned(ref, start):
        return jnp.concatenate([ref[:, start : start + LANES], filler], axis=0).T

    def choose(at, first, last):
        near[:, at] = jnp.where(odd_col, first, last)
        far[:, at] = jnp.where(odd_col, last, first)

    choose(slice(0, rows), left[...], right[...])
    for index, ref in enumerate((above, below)):
        first = turned(ref, 0)[0:8]
        last = turned(ref, cols - LANES)[LANES - 8 :]
        choose(slice(rows + index * LANES, rows + (index + 1) * LANES), first, last)


def corner_messages(flags, got_near, got_far, left, right):
    rows = left.shape[1]
    vmem = pl.BlockSpec(memory_space=pltpu.VMEM)
    shapes = [got_near.shape, got_near.shape, (8, rows + 2 * LANES), (8, rows + 2 * LANES)]
    return pl.pallas_call(
        corner_kernel,
        out_shape=[jax.ShapeDtypeStruct(shape, F32) for shape in shapes],
        in_specs=[pl.BlockSpec(memory_space=pltpu.SMEM)] + [vmem] * 4,
        out_specs=[vmem] * 4,
        compiler_params=params(2),
        cost_estimate=cost(1),
        name="corners",
    )(flags, got_near, got_far, left, right)


def raster_kernel(
    flags, b_hbm, k_hbm, above, below, got_near, got_far, tracts, county, pay, sums, two, four,
    bx, kx, v1, v2, v3, rows_b, rows_2, sems
):
    rows, cols = two.shape
    wide = cols + 2 * LANES
    inner = (slice(PAD, PAD + rows), slice(LANES, LANES + cols))
    copy_b = pltpu.make_async_copy(b_hbm, bx.at[inner], sems.at[0])
    copy_k = pltpu.make_async_copy(k_hbm, kx.at[inner], sems.at[1])
    copy_b.start()
    copy_k.start()
    odd = flags[5] > 0
    before = jnp.where(odd, got_near[...], got_far[...])
    after = jnp.where(odd, got_far[...], got_near[...])
    filler = jnp.zeros((LANES - 16, before.shape[1]), F32)
    turned = jnp.concatenate([after, filler, before], axis=0).T
    lane = iota((rows, LANES), 1)
    for ref, left, right, skip in (
        (bx, turned, turned, 0),
        (kx, pltpu.roll(turned, HALO, 1), pltpu.roll(turned, LANES - HALO, 1), HALO),
    ):
        ref[PAD - 8 : PAD, :] = jnp.zeros((8, wide), F32)
        ref[PAD + rows : PAD + rows + 8, :] = jnp.zeros((8, wide), F32)
        for start, part, keep in (
            (0, left, lane >= LANES - HALO),
            (LANES + cols, right, lane < HALO),
        ):
            own = slice(start, start + LANES)
            ref[PAD : PAD + rows, own] = jnp.where(keep, part[:rows], 0.0)
            keep = keep[:HALO]
            for place, at in ((PAD - HALO, rows), (PAD + rows, rows + LANES)):
                corner = turned[at + skip : at + skip + HALO]
                ref[place : place + HALO, own] = jnp.where(keep, corner, 0.0)
    for ref, part in ((bx, slice(0, HALO)), (kx, slice(HALO, 2 * HALO))):
        ref[PAD - HALO : PAD, inner[1]] = above[part, :]
        ref[PAD + rows : PAD + rows + HALO, inner[1]] = below[part, :]
    copy_b.wait()
    copy_k.wait()

    column, sub = iota((8, wide), 1), iota((8, wide), 0)
    inside = jnp.logical_and(
        jnp.logical_or(column >= LANES, flags[2] > 0),
        jnp.logical_or(column < LANES + cols, flags[3] > 0),
    )

    def apply(src, row):
        centre = src[pl.ds(row, 8), :]
        up, down = src[pl.ds(row - 1, 1), :], src[pl.ds(row + 8, 1), :]
        beside = jnp.where(sub == 0, up, pltpu.roll(centre, 1, 0))
        beside = beside + jnp.where(sub == 7, down, pltpu.roll(centre, 7, 0))
        beside = beside + (pltpu.roll(centre, 1, 1) + pltpu.roll(centre, wide - 1, 1))
        out = (4.0 + kx[pl.ds(row, 8), :]) * centre - beside
        return centre[:, inner[1]], jnp.where(inside, out, 0.0)

    def edges(src, dst):
        for row, flag in ((PAD - 8, flags[0]), (PAD + rows, flags[1])):
            _, out = apply(src, row)
            dst[row : row + 8, :] = jnp.where(flag > 0, out, 0.0)

    def fold(value):
        return jnp.sum(value, axis=0, keepdims=True)

    def sweep_one(step, carry):
        sum_0, sum_1 = carry
        total = jnp.zeros((8, cols), F32)
        for part in range(2):
            row = pl.multiple_of(PAD + step * BLOCK + 8 * part, 8)
            centre, out = apply(bx, row)
            v1[pl.ds(row, 8), :] = out
            out = out[:, inner[1]]
            sum_0, sum_1 = sum_0 + centre * centre, sum_1 + out * out
            total = total + centre
        rows_b[pl.ds(step, 1), :] = fold(total)
        return sum_0, sum_1

    def sweep_two(step, sum_2):
        total = jnp.zeros((8, cols), F32)
        for part in range(2):
            row = pl.multiple_of(PAD + step * BLOCK + 8 * part, 8)
            _, out = apply(v1, row)
            v2[pl.ds(row, 8), :] = out
            out = out[:, inner[1]]
            two[pl.ds(row - PAD, 8), :] = out
            sum_2 = sum_2 + out * out
            total = total + out
        rows_2[pl.ds(step, 1), :] = fold(total)
        return sum_2

    def sweep_three(step, sum_3):
        row = pl.multiple_of(PAD + step * 8, 8)
        _, out = apply(v2, row)
        v3[pl.ds(row, 8), :] = out
        out = out[:, inner[1]]
        return sum_3 + out * out

    def sweep_four(step, carry):
        row = pl.multiple_of(PAD + step * 8, 8)
        _, out = apply(v3, row)
        four[pl.ds(row - PAD, 8), :] = out[:, inner[1]]
        return carry

    zero = jnp.zeros((8, cols), F32)
    edges(bx, v1)
    sum_0, sum_1 = lax.fori_loop(0, rows // BLOCK, sweep_one, (zero, zero), unroll=4)
    edges(v1, v2)
    sum_2 = lax.fori_loop(0, rows // BLOCK, sweep_two, zero, unroll=4)
    edges(v2, v3)
    sum_3 = lax.fori_loop(0, rows // 8, sweep_three, zero, unroll=8)
    lax.fori_loop(0, rows // 8, sweep_four, 0, unroll=8)

    pay[...] = jnp.zeros(pay.shape, F32)
    for index, value in enumerate((sum_0, sum_1, sum_2, sum_3)):
        value = fold(value)
        folded = value[:, :LANES]
        for start in range(LANES, cols, LANES):
            folded = folded + value[:, start : start + LANES]
        pay[8 + index : 9 + index, :] = folded

    group, place = iota((cols, LANES), 0) // BLOCK, iota((cols, LANES), 1)
    blocks = dot(rows_b[...], jnp.where(group == place, 1.0, 0.0))
    blocks = blocks + dot(rows_2[...], jnp.where(group + cols // BLOCK == place, 1.0, 0.0))
    for tract in range(TRACTS_DEV):
        sums[tract : tract + 1, :] = fold(jnp.where(tracts[...] == tract, blocks, 0.0))
    totals = sums[...]
    first = iota(totals.shape, 1) < cols // BLOCK
    for index, keep in enumerate((first, jnp.logical_not(first))):
        total = jnp.sum(jnp.where(keep, totals, 0.0), axis=1, keepdims=True)
        match = county[...] == iota((TRACTS_DEV, COUNTIES), 1)
        by_county = fold(jnp.where(match, total, 0.0))
        for part in range(COUNTIES // LANES):
            pay[4 * index + part : 4 * index + part + 1, :] = by_county[
                :, part * LANES : (part + 1) * LANES
            ]


def raster(flags, b, kappa, above, below, got_near, got_far, tracts, county):
    rows, cols = b.shape
    shape = (rows + 2 * PAD, cols + 2 * LANES)
    any_spec = pl.BlockSpec(memory_space=pl.ANY)
    vmem = pl.BlockSpec(memory_space=pltpu.VMEM)
    return pl.pallas_call(
        raster_kernel,
        out_shape=(
            jax.ShapeDtypeStruct((16, LANES), F32),
            jax.ShapeDtypeStruct((TRACTS_DEV, LANES), F32),
            jax.ShapeDtypeStruct(b.shape, F32),
            jax.ShapeDtypeStruct(b.shape, F32),
        ),
        in_specs=[pl.BlockSpec(memory_space=pltpu.SMEM), any_spec, any_spec] + [vmem] * 6,
        out_specs=(vmem, vmem, vmem, vmem),
        scratch_shapes=[pltpu.VMEM(shape, F32)] * 5
        + [pltpu.VMEM((rows // BLOCK, cols), F32)] * 2
        + [pltpu.SemaphoreType.DMA((2,))],
        compiler_params=params(60),
        cost_estimate=cost(1),
        name="raster",
    )(flags, b, kappa, above, below, got_near, got_far, tracts, county)


def two_sum(a, b):
    s = a + b
    t = s - a
    return s, (a - (s - t)) + (b - t)


def two_prod(a, b):
    def split(x):
        big = x * 4097.0
        high = big - (big - x)
        return high, x - high

    product = a * b
    a_high, a_low = split(a)
    b_high, b_low = split(b)
    low = ((a_high * b_high - product) + a_high * b_low + a_low * b_high) + a_low * b_low
    return product, low


def pair_add(a, b):
    high, low = two_sum(a[0], b[0])
    return two_sum(high, low + (a[1] + b[1]))


def pair_mul(a, b):
    high, low = two_prod(a[0], b[0])
    return two_sum(high, low + (a[0] * b[1] + a[1] * b[0]))


def pair_cross(a, b, c, d):
    minus = pair_mul(c, d)
    high, low = pair_add(pair_mul(a, b), (-minus[0], -minus[1]))
    return high + low


def finish_kernel(devices, got, sums, state, b, two, four, solution, residual, tract, county, states, scal):
    @pl.when(pl.program_id(0) == 0)
    def _():
        whole = got[0:16, :]
        err = jnp.zeros_like(whole)
        for device in range(1, devices):
            whole, low = two_sum(whole, got[16 * device : 16 * device + 16, :])
            err = err + low
        pair = (whole[8:12, :], err[8:12, :])
        shift = LANES // 2
        while shift:
            pair = pair_add(pair, (pltpu.roll(pair[0], shift, 1), pltpu.roll(pair[1], shift, 1)))
            shift //= 2
        scale = 1.0 / pair[0][0:1, :]
        m = []
        for index in range(4):
            m.append(pair_mul((scale, jnp.zeros_like(scale)), (pair[0][index : index + 1, :], pair[1][index : index + 1, :])))
        below = pair_cross(m[1], m[3], m[2], m[2])
        c_0 = pair_cross(m[0], m[3], m[1], m[2]) / below
        c_1 = pair_cross(m[0], m[2], m[1], m[1]) / below
        scal[0:1, :] = c_0
        scal[1:2, :] = c_1
        by_county = c_0 * whole[0:4, :] - c_1 * whole[4:8, :]
        county[...] = by_county
        place = iota((64, LANES), 0)
        total = jnp.zeros((64, LANES), F32)
        for part in range(COUNTIES // LANES):
            total = total + jnp.where(state[part : part + 1, :] == place, by_county[part : part + 1, :], 0.0)
        states[...] = dot(jnp.ones((8, LANES), F32), total, (1, 1))[0:1, :]
        first = iota((1, LANES), 1) < LANES // 2
        mixed = jnp.where(first, c_0, -c_1) * sums[...]
        tract[...] = dot(jnp.ones((8, LANES), F32), mixed, (1, 1))[0:1, :]

    c_0, c_1 = scal[0:1, 0:1], scal[1:2, 0:1]
    solution[...] = c_0 * b[...] - c_1 * two[...]
    residual[...] = b[...] - c_0 * two[...] + c_1 * four[...]


def finish(got, sums, state, b, two, four):
    rows, cols = b.shape
    step = 256
    devices = got.shape[0] // 16

    def fixed(shape):
        return pl.BlockSpec(shape, lambda i: (0, 0))

    tile = pl.BlockSpec((step, cols), lambda i: (i, 0))
    small = [(1, 64), (COUNTIES // LANES, LANES), (1, 64)]
    return pl.pallas_call(
        functools.partial(finish_kernel, devices),
        grid=(rows // step,),
        out_shape=[jax.ShapeDtypeStruct(b.shape, F32)] * 2
        + [jax.ShapeDtypeStruct(shape, F32) for shape in small],
        in_specs=[fixed(got.shape), fixed(sums.shape), fixed(state.shape), tile, tile, tile],
        out_specs=[tile, tile] + [fixed(shape) for shape in small],
        scratch_shapes=[pltpu.VMEM((8, LANES), F32)],
        compiler_params=params(60),
        cost_estimate=cost(8),
        name="finish",
    )(got, sums, state, b, two, four)


def invert_pair(a, b, c):
    scale = 1.0 / (a * c - b * b)
    return c * scale, -b * scale, a * scale


def invert_block(rows):
    size = LANES
    lane, sub = iota((8, size), 1), iota((8, size), 0)
    groups = size // 8
    pivots = [jnp.ones((8, size), F32)] * groups
    for k in range(0, size, 4):
        g, s = divmod(k, 8)
        block = jnp.logical_and(lane >= k, lane < k + 4)
        factors = {
            h: [jnp.broadcast_to(rows[h][:, k + c : k + c + 1], (8, size)) for c in range(4)]
            for h in range(g, groups)
        }

        def at(i, j):
            return jnp.broadcast_to(factors[g][j][s + i : s + i + 1, :], (8, size))

        line = []
        for i in range(4):
            whole = jnp.broadcast_to(rows[g][s + i : s + i + 1, :], (8, size))
            line.append(jnp.where(block, jnp.where(lane == k + i, 1.0, 0.0), whole))
        p00, p10, p11 = at(0, 0), at(1, 0), at(1, 1)
        q00, q01, q10, q11 = at(2, 0), at(2, 1), at(3, 0), at(3, 1)
        i00, i10, i11 = invert_pair(p00, p10, p11)
        t00, t01 = q00 * i00 + q01 * i10, q00 * i10 + q01 * i11
        t10, t11 = q10 * i00 + q11 * i10, q10 * i10 + q11 * i11
        c00 = at(2, 2) - (t00 * q00 + t01 * q01)
        c10 = at(3, 2) - (t10 * q00 + t11 * q01)
        c11 = at(3, 3) - (t10 * q10 + t11 * q11)
        j00, j10, j11 = invert_pair(c00, c10, c11)
        low_2 = line[2] - (t00 * line[0] + t01 * line[1])
        low_3 = line[3] - (t10 * line[0] + t11 * line[1])
        w_2, w_3 = j00 * low_2 + j10 * low_3, j10 * low_2 + j11 * low_3
        w_0 = (i00 * line[0] + i10 * line[1]) - (t00 * w_2 + t10 * w_3)
        w_1 = (i10 * line[0] + i11 * line[1]) - (t01 * w_2 + t11 * w_3)
        for h in range(g, groups):
            f = factors[h]
            cut = (f[0] * w_0 + f[1] * w_1) + (f[2] * w_2 + f[3] * w_3)
            updated = jnp.where(block, 0.0, rows[h]) - cut
            if h > g:
                rows[h] = updated
                continue
            l10, l32 = p10 / p00, c10 / c00
            done = (line[0], line[1] - l10 * line[0], low_2, low_3 - l32 * low_2)
            diagonal = (p00, p11 - l10 * p10, c00, c11 - l32 * c10)
            own = jnp.where(sub >= s + 4, updated, rows[g])
            pivot = pivots[g]
            for i in range(4):
                own = jnp.where(sub == s + i, done[i], own)
                pivot = jnp.where(sub == s + i, diagonal[i], pivot)
            rows[g], pivots[g] = own, pivot
    out = []
    for g in range(groups):
        kept = jnp.where(lane <= sub + 8 * g, rows[g], 0.0)
        out.append(kept / jnp.sqrt(pivots[g]))
    return out


def factor_kernel(a, inverse, part, left):
    size = LANES
    part[...] = a[0:size, 0:size]
    inverse[0:size, size:] = jnp.zeros((size, size), F32)

    def body(index, carry):
        rows = [part[8 * g : 8 * g + 8, :] for g in range(size // 8)]
        rows = invert_block(rows)
        for g in range(size // 8):
            part[8 * g : 8 * g + 8, :] = rows[g]

        @pl.when(index == 0)
        def _():
            first = part[...]
            inverse[0:size, 0:size] = first
            left[...] = dot(a[size:, 0:size], first, (1, 1))
            part[...] = a[size:, size:] - dot(left[...], left[...], (1, 1))

        return carry

    lax.fori_loop(0, 2, body, 0)
    inverse[size:, size:] = part[...]
    inverse[size:, 0:size] = -dot(part[...], dot(left[...], inverse[0:size, 0:size]))


def factor(a):
    size = a.shape[0]
    half = pltpu.VMEM((LANES, LANES), F32)
    return pl.pallas_call(
        factor_kernel,
        out_shape=jax.ShapeDtypeStruct(a.shape, F32),
        in_specs=[pl.BlockSpec(memory_space=pltpu.VMEM)],
        out_specs=pl.BlockSpec(memory_space=pltpu.VMEM),
        scratch_shapes=[half, half],
        compiler_params=params(60),
        cost_estimate=cost(1),
        name="factor",
    )(a)


def split(value):
    high = value.astype(jnp.bfloat16)
    return high, (value - high.astype(F32)).astype(jnp.bfloat16)


def tile_rows(ref, index, size, count):
    parts = [
        ref[pl.ds(part * count + index, size, stride=count * (size // LANES)), :]
        for part in range(size // LANES)
    ]
    return jnp.concatenate(parts, axis=1)


def update_kernel(flags, column, column_got, wide_hbm, wide_got, inverse, schur, panel, updated, wide, other, sem):
    size = inverse.shape[0]
    count = other.shape[0]

    @pl.when(pl.program_id(0) == 0)
    def _():
        @pl.when(flags[4] > 0)
        def _():
            pltpu.make_async_copy(wide_got, wide, sem).start()

        @pl.when(flags[4] == 0)
        def _():
            pltpu.make_async_copy(wide_hbm, wide, sem).start()

        pltpu.make_async_copy(wide_hbm, wide, sem).wait()
        for index in range(count):
            high, low = split(dot(inverse[...], tile_rows(wide, index, size, count)))
            other[index, 0:size, :] = high
            other[index, size : 2 * size, :] = low
            other[index, 2 * size :, :] = high

    own = jnp.where(flags[5] > 0, column_got[0], column[0])
    own = dot(own, inverse[...], (1, 1))
    panel[0] = own
    high, low = split(own)
    lhs = jnp.concatenate([high, high, low], axis=1)
    for index in range(count):
        product = jnp.dot(lhs, other[index], preferred_element_type=F32)
        for part in range(size // LANES):
            at = pl.ds(part * count + index, size, stride=count * (size // LANES))
            updated[0, at, :] = schur[0, at, :] - product[:, part * LANES : (part + 1) * LANES]


def update(flags, column, column_got, wide, wide_got, inverse, schur):
    count_rows, size, count, _ = schur.shape
    parts = size // LANES
    flat = lane_tiles(schur)

    def step(*block):
        return pl.BlockSpec((1,) + block, lambda i: (i,) + (0,) * len(block))

    any_spec = pl.BlockSpec(memory_space=pl.ANY)
    inverse_spec = pl.BlockSpec(inverse.shape, lambda i: (0, 0))
    panel, updated = pl.pallas_call(
        update_kernel,
        grid=(count_rows,),
        out_shape=(
            jax.ShapeDtypeStruct(column.shape, F32),
            jax.ShapeDtypeStruct(flat.shape, F32),
        ),
        in_specs=[pl.BlockSpec(memory_space=pltpu.SMEM), step(size, size), step(size, size)]
        + [any_spec, any_spec, inverse_spec, step(*flat.shape[1:])],
        out_specs=(step(size, size), step(*flat.shape[1:])),
        scratch_shapes=[
            pltpu.VMEM(wide.shape, F32),
            pltpu.VMEM((count, 3 * size, size), jnp.bfloat16),
            pltpu.SemaphoreType.DMA,
        ],
        compiler_params=params(60),
        cost_estimate=cost(17),
        name="update",
    )(flags, column, column_got, wide, wide_got, inverse, flat)
    updated = updated.reshape(count_rows, size, parts, count, LANES).transpose(0, 1, 3, 2, 4)
    return panel, updated.reshape(schur.shape)


def per_device(right_side, kappa_sq, block_tract, tract_county, county_state, schur):
    n_row, n_col = lax.axis_size("row"), lax.axis_size("col")
    row, col = lax.axis_index("row"), lax.axis_index("col")
    flags = [row > 0, row < n_row - 1, col > 0, col < n_col - 1, row % 2 == 1, col % 2 == 1]
    flags = jnp.stack(flags).astype(jnp.int32)

    corner = corner_block(schur)
    steps = small_steps(n_row, n_col)
    corner = small_hop(corner, steps[0])
    near, far, left, right = edge_messages(flags, right_side, kappa_sq)
    near, far = trade(near, far, "row")
    near, far, corner = lax.optimization_barrier((near, far, corner))
    corner = small_hop(corner, steps[1])
    above, below, near, far = corner_messages(flags, near, far, left, right)
    near, far = trade(near, far, "col")
    near, far, corner = lax.optimization_barrier((near, far, corner))
    corner = small_hop(corner, steps[2])
    held, flat, near = lax.optimization_barrier((schur, lane_tiles(schur), near))
    column, wide = extract(held, flat)
    column, wide, corner = lax.optimization_barrier((column, wide, corner))
    column_got, wide_got = hop(column, "col", n_col), hop(wide, "row", n_row)
    for step in steps[3:]:
        corner = small_hop(corner, step)
    near, far, corner = lax.optimization_barrier((near, far, corner))

    tracts = jnp.concatenate([block_tract, block_tract], axis=1)
    pay, sums, two, four = raster(
        flags, right_side, kappa_sq, above, below, near, far, tracts, tract_county[:, None]
    )
    pay, column_got, wide_got = lax.optimization_barrier((pay, column_got, wide_got))
    got = exchange(pay).reshape(-1, LANES)
    stride = n_col
    while stride > 2:
        column = merge(column_got, column, "col", stride)
        stride //= 2
        column_got = hop(column, "col", stride)
    stride = n_row
    wide = merge(wide_got, wide, "row", stride)
    stride //= 2
    wide_got = hop(wide, "row", stride)
    inverse = factor(corner)
    wide_got, got, inverse, column_got = lax.optimization_barrier((wide_got, got, inverse, column_got))
    while stride > 2:
        wide = merge(wide_got, wide, "row", stride)
        stride //= 2
        wide_got = hop(wide, "row", stride)
    solution, residual, tract_totals, county_totals, state_totals = finish(
        got,
        sums,
        county_state.reshape(COUNTIES // LANES, LANES),
        right_side,
        two,
        four,
    )
    panel, updated = update(flags, column, column_got, wide, wide_got, inverse, schur)
    return (
        solution,
        residual,
        tract_totals.reshape(-1)[:TRACTS_DEV],
        county_totals.reshape(-1),
        state_totals.reshape(-1)[:STATES],
        updated,
        panel,
    )


def solution(mesh):
    in_specs = (
        P("row", "col"),
        P("row", "col"),
        P("row", "col"),
        P(("row", "col")),
        P(),
        P(None, "row", None, "col"),
    )
    out_specs = (
        P("row", "col"),
        P("row", "col"),
        P(("row", "col")),
        P(),
        P(),
        P(None, "row", None, "col"),
        P(None, "row", None),
    )
    return jax.shard_map(
        per_device, mesh=mesh, in_specs=in_specs, out_specs=out_specs, check_vma=False
    )
```

```python
import functools
import jax
import jax.numpy as jnp
from jax import lax
from jax.experimental import pallas as pl
from jax.experimental.pallas import tpu as pltpu
from jax.sharding import PartitionSpec as P

BLOCK = 16
TRACTS_DEV = 64
COUNTIES = 512
STATES = 56
HALO = 4
PAD = 16
LANES = 128
HIGHEST = lax.Precision.HIGHEST
F32 = jnp.float32


def iota(shape, dim):
    return lax.broadcasted_iota(jnp.int32, shape, dim)


def dot(a, b, contract=(1, 0)):
    dims = (((contract[0],), (contract[1],)), ((), ()))
    return lax.dot_general(a, b, dims, precision=HIGHEST, preferred_element_type=F32)


def cost(micros):
    return pl.CostEstimate(flops=micros * 10**9, transcendentals=0, bytes_accessed=1 << 10)


def params(mib):
    return pltpu.CompilerParams(vmem_limit_bytes=mib << 20)


def trade(near, far, axis):
    size = lax.axis_size(axis)
    inside = [(i, i ^ 1) for i in range(size)]
    between = [(i, i + 1) for i in range(1, size - 1, 2)]
    between = between + [(j, i) for i, j in between]
    return lax.ppermute(near, axis, inside), lax.ppermute(far, axis, between)


def after(value, *others):
    return lax.optimization_barrier((value,) + others)[0]


def hop(block, axis, stride):
    pairs = [(i, i + stride // 2) for i in range(0, lax.axis_size(axis), stride)]
    return lax.ppermute(block, axis, pairs)


def relay(source, held, target, sem):
    copy = pltpu.make_async_copy(source, held, sem)
    copy.start()
    copy.wait()
    copy = pltpu.make_async_copy(held, target, sem)
    copy.start()
    copy.wait()


def merge_kernel(flag, got, _, out, held, sem):
    @pl.when(flag[0] > 0)
    def _():
        relay(got, held, out, sem)


def merge(got, block, axis, stride):
    flag = (lax.axis_index(axis) % stride == stride // 2).astype(jnp.int32).reshape(1)
    any_spec = pl.BlockSpec(memory_space=pl.ANY)
    return pl.pallas_call(
        merge_kernel,
        out_shape=jax.ShapeDtypeStruct(block.shape, block.dtype),
        in_specs=[pl.BlockSpec(memory_space=pltpu.SMEM), any_spec, any_spec],
        out_specs=any_spec,
        scratch_shapes=[pltpu.VMEM(block.shape, F32), pltpu.SemaphoreType.DMA],
        input_output_aliases={2: 0},
        compiler_params=params(60),
        cost_estimate=cost(2),
        name="merge",
    )(flag, got, block)


def lane_tiles(schur):
    count_rows, size, count, width = schur.shape
    parts = width // LANES
    flat = schur.reshape(count_rows, size, count, parts, LANES).transpose(0, 1, 3, 2, 4)
    return flat.reshape(count_rows, size * parts * count, LANES)


def extract_kernel(schur, flat, raw, wide, held_raw, held_wide, sems):
    parts = ((schur.at[:, :, 0, :], held_raw, raw), (flat.at[0], held_wide, wide))
    loads = [pltpu.make_async_copy(a, b, sems.at[i]) for i, (a, b, _) in enumerate(parts)]
    stores = [pltpu.make_async_copy(b, c, sems.at[2 + i]) for i, (_, b, c) in enumerate(parts)]
    for copy in loads:
        copy.start()
    for load, store in zip(loads, stores):
        load.wait()
        store.start()
    for copy in stores:
        copy.wait()


def corner_block_kernel(schur, corner, sem):
    copy = pltpu.make_async_copy(schur.at[0, :, 0, :], corner, sem)
    copy.start()
    copy.wait()


def corner_block(schur):
    size = schur.shape[1]
    return pl.pallas_call(
        corner_block_kernel,
        out_shape=jax.ShapeDtypeStruct((size, size), F32),
        in_specs=[pl.BlockSpec(memory_space=pl.ANY)],
        out_specs=pl.BlockSpec(memory_space=pltpu.VMEM),
        scratch_shapes=[pltpu.SemaphoreType.DMA],
        compiler_params=params(60),
        cost_estimate=cost(2),
        name="corner",
    )(schur)


def extract(schur, flat):
    count_rows, size, _, _ = schur.shape
    any_spec = pl.BlockSpec(memory_space=pl.ANY)
    return pl.pallas_call(
        extract_kernel,
        out_shape=(
            jax.ShapeDtypeStruct((count_rows, size, size), F32),
            jax.ShapeDtypeStruct(flat.shape[1:], F32),
        ),
        in_specs=[any_spec, any_spec],
        out_specs=(any_spec, any_spec),
        scratch_shapes=[
            pltpu.VMEM((count_rows, size, size), F32),
            pltpu.VMEM(flat.shape[1:], F32),
            pltpu.SemaphoreType.DMA((4,)),
        ],
        compiler_params=params(60),
        cost_estimate=cost(3),
        name="extract",
    )(schur, flat)


def small_steps(n_row, n_col):
    steps = []
    for axis, stride in (("col", n_col), ("row", n_row)):
        while stride > 1:
            steps.append((axis, stride))
            stride //= 2
    return steps


def small_hop(block, step):
    axis, stride = step
    got = hop(block, axis, stride)
    return jnp.where(lax.axis_index(axis) % stride == stride // 2, got, block)


def exchange(mine):
    axes = ("row", "col")
    devices = lax.axis_size("row") * lax.axis_size("col")
    return lax.all_to_all(jnp.broadcast_to(mine, (devices,) + mine.shape), axes, 0, 0)


def edge_kernel(flags, b_top, b_low, k_top, k_low, b_left, b_right, k_left, k_right, near, far, left, right):
    odd = flags[4] > 0
    for part, top, low in ((slice(0, HALO), b_top, b_low), (slice(HALO, 2 * HALO), k_top, k_low)):
        first, last = top[0:HALO, :], low[8 - HALO : 8, :]
        near[part, :] = jnp.where(odd, first, last)
        far[part, :] = jnp.where(odd, last, first)
    left[0:HALO, :] = b_left[...].T[0:HALO]
    left[HALO:, :] = k_left[...].T[0:HALO]
    right[0:HALO, :] = k_right[...].T[LANES - HALO :]
    right[HALO:, :] = b_right[...].T[LANES - HALO :]


def edge_messages(flags, b, kappa):
    rows, cols = b.shape

    def spec(shape, row, col):
        return pl.BlockSpec(shape, lambda i: (row, col))

    ends = [spec((8, cols), 0, 0), spec((8, cols), rows // 8 - 1, 0)]
    sides = [spec((rows, LANES), 0, 0), spec((rows, LANES), 0, cols // LANES - 1)]
    shapes = [(8, cols), (8, cols), (8, rows), (8, rows)]
    return pl.pallas_call(
        edge_kernel,
        grid=(1,),
        out_shape=[jax.ShapeDtypeStruct(shape, F32) for shape in shapes],
        in_specs=[pl.BlockSpec(memory_space=pltpu.SMEM)] + ends * 2 + sides * 2,
        out_specs=[spec(shape, 0, 0) for shape in shapes],
        compiler_params=params(60),
        cost_estimate=cost(2),
        name="edges",
    )(flags, b, b, kappa, kappa, b, b, kappa, kappa)


def corner_kernel(flags, got_near, got_far, left, right, above, below, near, far):
    odd, odd_col = flags[4] > 0, flags[5] > 0
    above[...] = jnp.where(odd, got_near[...], got_far[...])
    below[...] = jnp.where(odd, got_far[...], got_near[...])
    cols, rows = above.shape[1], left.shape[1]
    filler = jnp.zeros((LANES - 8, LANES), F32)

    def turned(ref, start):
        return jnp.concatenate([ref[:, start : start + LANES], filler], axis=0).T

    def choose(at, first, last):
        near[:, at] = jnp.where(odd_col, first, last)
        far[:, at] = jnp.where(odd_col, last, first)

    choose(slice(0, rows), left[...], right[...])
    for index, ref in enumerate((above, below)):
        first = turned(ref, 0)[0:8]
        last = turned(ref, cols - LANES)[LANES - 8 :]
        choose(slice(rows + index * LANES, rows + (index + 1) * LANES), first, last)


def corner_messages(flags, got_near, got_far, left, right):
    rows = left.shape[1]
    vmem = pl.BlockSpec(memory_space=pltpu.VMEM)
    shapes = [got_near.shape, got_near.shape, (8, rows + 2 * LANES), (8, rows + 2 * LANES)]
    return pl.pallas_call(
        corner_kernel,
        out_shape=[jax.ShapeDtypeStruct(shape, F32) for shape in shapes],
        in_specs=[pl.BlockSpec(memory_space=pltpu.SMEM)] + [vmem] * 4,
        out_specs=[vmem] * 4,
        compiler_params=params(2),
        cost_estimate=cost(1),
        name="corners",
    )(flags, got_near, got_far, left, right)


def raster_kernel(
    flags, b_hbm, k_hbm, above, below, got_near, got_far, tracts, county, pay, sums, two, four,
    bx, kx, v1, v2, v3, rows_b, rows_2, sems
):
    rows, cols = two.shape
    wide = cols + 2 * LANES
    inner = (slice(PAD, PAD + rows), slice(LANES, LANES + cols))
    copy_b = pltpu.make_async_copy(b_hbm, bx.at[inner], sems.at[0])
    copy_k = pltpu.make_async_copy(k_hbm, kx.at[inner], sems.at[1])
    copy_b.start()
    copy_k.start()
    odd = flags[5] > 0
    before = jnp.where(odd, got_near[...], got_far[...])
    after = jnp.where(odd, got_far[...], got_near[...])
    filler = jnp.zeros((LANES - 16, before.shape[1]), F32)
    turned = jnp.concatenate([after, filler, before], axis=0).T
    lane = iota((rows, LANES), 1)
    for ref, left, right, skip in (
        (bx, turned, turned, 0),
        (kx, pltpu.roll(turned, HALO, 1), pltpu.roll(turned, LANES - HALO, 1), HALO),
    ):
        ref[PAD - 8 : PAD, :] = jnp.zeros((8, wide), F32)
        ref[PAD + rows : PAD + rows + 8, :] = jnp.zeros((8, wide), F32)
        for start, part, keep in (
            (0, left, lane >= LANES - HALO),
            (LANES + cols, right, lane < HALO),
        ):
            own = slice(start, start + LANES)
            ref[PAD : PAD + rows, own] = jnp.where(keep, part[:rows], 0.0)
            keep = keep[:HALO]
            for place, at in ((PAD - HALO, rows), (PAD + rows, rows + LANES)):
                corner = turned[at + skip : at + skip + HALO]
                ref[place : place + HALO, own] = jnp.where(keep, corner, 0.0)
    for ref, part in ((bx, slice(0, HALO)), (kx, slice(HALO, 2 * HALO))):
        ref[PAD - HALO : PAD, inner[1]] = above[part, :]
        ref[PAD + rows : PAD + rows + HALO, inner[1]] = below[part, :]
    copy_b.wait()
    copy_k.wait()

    column, sub = iota((8, wide), 1), iota((8, wide), 0)
    inside = jnp.logical_and(
        jnp.logical_or(column >= LANES, flags[2] > 0),
        jnp.logical_or(column < LANES + cols, flags[3] > 0),
    )

    def apply(src, row):
        centre = src[pl.ds(row, 8), :]
        up, down = src[pl.ds(row - 1, 1), :], src[pl.ds(row + 8, 1), :]
        beside = jnp.where(sub == 0, up, pltpu.roll(centre, 1, 0))
        beside = beside + jnp.where(sub == 7, down, pltpu.roll(centre, 7, 0))
        beside = beside + (pltpu.roll(centre, 1, 1) + pltpu.roll(centre, wide - 1, 1))
        out = (4.0 + kx[pl.ds(row, 8), :]) * centre - beside
        return centre[:, inner[1]], jnp.where(inside, out, 0.0)

    def edges(src, dst):
        for row, flag in ((PAD - 8, flags[0]), (PAD + rows, flags[1])):
            _, out = apply(src, row)
            dst[row : row + 8, :] = jnp.where(flag > 0, out, 0.0)

    def fold(value):
        return jnp.sum(value, axis=0, keepdims=True)

    def sweep_one(step, carry):
        sum_0, sum_1 = carry
        total = jnp.zeros((8, cols), F32)
        for part in range(2):
            row = pl.multiple_of(PAD + step * BLOCK + 8 * part, 8)
            centre, out = apply(bx, row)
            v1[pl.ds(row, 8), :] = out
            out = out[:, inner[1]]
            sum_0, sum_1 = sum_0 + centre * centre, sum_1 + out * out
            total = total + centre
        rows_b[pl.ds(step, 1), :] = fold(total)
        return sum_0, sum_1

    def sweep_two(step, sum_2):
        total = jnp.zeros((8, cols), F32)
        for part in range(2):
            row = pl.multiple_of(PAD + step * BLOCK + 8 * part, 8)
            _, out = apply(v1, row)
            v2[pl.ds(row, 8), :] = out
            out = out[:, inner[1]]
            two[pl.ds(row - PAD, 8), :] = out
            sum_2 = sum_2 + out * out
            total = total + out
        rows_2[pl.ds(step, 1), :] = fold(total)
        return sum_2

    def sweep_three(step, sum_3):
        row = pl.multiple_of(PAD + step * 8, 8)
        _, out = apply(v2, row)
        v3[pl.ds(row, 8), :] = out
        out = out[:, inner[1]]
        return sum_3 + out * out

    def sweep_four(step, carry):
        row = pl.multiple_of(PAD + step * 8, 8)
        _, out = apply(v3, row)
        four[pl.ds(row - PAD, 8), :] = out[:, inner[1]]
        return carry

    zero = jnp.zeros((8, cols), F32)
    edges(bx, v1)
    sum_0, sum_1 = lax.fori_loop(0, rows // BLOCK, sweep_one, (zero, zero), unroll=8)
    edges(v1, v2)
    sum_2 = lax.fori_loop(0, rows // BLOCK, sweep_two, zero, unroll=8)
    edges(v2, v3)
    sum_3 = lax.fori_loop(0, rows // 8, sweep_three, zero, unroll=16)
    lax.fori_loop(0, rows // 8, sweep_four, 0, unroll=16)

    pay[...] = jnp.zeros(pay.shape, F32)
    for index, value in enumerate((sum_0, sum_1, sum_2, sum_3)):
        value = fold(value)
        folded = value[:, :LANES]
        for start in range(LANES, cols, LANES):
            folded = folded + value[:, start : start + LANES]
        pay[8 + index : 9 + index, :] = folded

    group, place = iota((cols, LANES), 0) // BLOCK, iota((cols, LANES), 1)
    blocks = dot(rows_b[...], jnp.where(group == place, 1.0, 0.0))
    blocks = blocks + dot(rows_2[...], jnp.where(group + cols // BLOCK == place, 1.0, 0.0))
    for tract in range(TRACTS_DEV):
        sums[tract : tract + 1, :] = fold(jnp.where(tracts[...] == tract, blocks, 0.0))
    totals = sums[...]
    first = iota(totals.shape, 1) < cols // BLOCK
    for index, keep in enumerate((first, jnp.logical_not(first))):
        total = jnp.sum(jnp.where(keep, totals, 0.0), axis=1, keepdims=True)
        match = county[...] == iota((TRACTS_DEV, COUNTIES), 1)
        by_county = fold(jnp.where(match, total, 0.0))
        for part in range(COUNTIES // LANES):
            pay[4 * index + part : 4 * index + part + 1, :] = by_county[
                :, part * LANES : (part + 1) * LANES
            ]


def raster(flags, b, kappa, above, below, got_near, got_far, tracts, county):
    rows, cols = b.shape
    shape = (rows + 2 * PAD, cols + 2 * LANES)
    any_spec = pl.BlockSpec(memory_space=pl.ANY)
    vmem = pl.BlockSpec(memory_space=pltpu.VMEM)
    return pl.pallas_call(
        raster_kernel,
        out_shape=(
            jax.ShapeDtypeStruct((16, LANES), F32),
            jax.ShapeDtypeStruct((TRACTS_DEV, LANES), F32),
            jax.ShapeDtypeStruct(b.shape, F32),
            jax.ShapeDtypeStruct(b.shape, F32),
        ),
        in_specs=[pl.BlockSpec(memory_space=pltpu.SMEM), any_spec, any_spec] + [vmem] * 6,
        out_specs=(vmem, vmem, vmem, vmem),
        scratch_shapes=[pltpu.VMEM(shape, F32)] * 5
        + [pltpu.VMEM((rows // BLOCK, cols), F32)] * 2
        + [pltpu.SemaphoreType.DMA((2,))],
        compiler_params=params(60),
        cost_estimate=cost(1),
        name="raster",
    )(flags, b, kappa, above, below, got_near, got_far, tracts, county)


def two_sum(a, b):
    s = a + b
    t = s - a
    return s, (a - (s - t)) + (b - t)


def two_prod(a, b):
    def split(x):
        big = x * 4097.0
        high = big - (big - x)
        return high, x - high

    product = a * b
    a_high, a_low = split(a)
    b_high, b_low = split(b)
    low = ((a_high * b_high - product) + a_high * b_low + a_low * b_high) + a_low * b_low
    return product, low


def pair_add(a, b):
    high, low = two_sum(a[0], b[0])
    return two_sum(high, low + (a[1] + b[1]))


def pair_mul(a, b):
    high, low = two_prod(a[0], b[0])
    return two_sum(high, low + (a[0] * b[1] + a[1] * b[0]))


def pair_cross(a, b, c, d):
    minus = pair_mul(c, d)
    high, low = pair_add(pair_mul(a, b), (-minus[0], -minus[1]))
    return high + low


def finish_kernel(devices, got, sums, state, b, two, four, solution, residual, tract, county, states, scal):
    @pl.when(pl.program_id(0) == 0)
    def _():
        whole = got[0:16, :]
        err = jnp.zeros_like(whole)
        for device in range(1, devices):
            whole, low = two_sum(whole, got[16 * device : 16 * device + 16, :])
            err = err + low
        pair = (whole[8:12, :], err[8:12, :])
        shift = LANES // 2
        while shift:
            pair = pair_add(pair, (pltpu.roll(pair[0], shift, 1), pltpu.roll(pair[1], shift, 1)))
            shift //= 2
        scale = 1.0 / pair[0][0:1, :]
        m = []
        for index in range(4):
            m.append(pair_mul((scale, jnp.zeros_like(scale)), (pair[0][index : index + 1, :], pair[1][index : index + 1, :])))
        below = pair_cross(m[1], m[3], m[2], m[2])
        c_0 = pair_cross(m[0], m[3], m[1], m[2]) / below
        c_1 = pair_cross(m[0], m[2], m[1], m[1]) / below
        scal[0:1, :] = c_0
        scal[1:2, :] = c_1
        by_county = c_0 * whole[0:4, :] - c_1 * whole[4:8, :]
        county[...] = by_county
        place = iota((64, LANES), 0)
        total = jnp.zeros((64, LANES), F32)
        for part in range(COUNTIES // LANES):
            total = total + jnp.where(state[part : part + 1, :] == place, by_county[part : part + 1, :], 0.0)
        states[...] = dot(jnp.ones((8, LANES), F32), total, (1, 1))[0:1, :]
        first = iota((1, LANES), 1) < LANES // 2
        mixed = jnp.where(first, c_0, -c_1) * sums[...]
        tract[...] = dot(jnp.ones((8, LANES), F32), mixed, (1, 1))[0:1, :]

    c_0, c_1 = scal[0:1, 0:1], scal[1:2, 0:1]
    solution[...] = c_0 * b[...] - c_1 * two[...]
    residual[...] = b[...] - c_0 * two[...] + c_1 * four[...]


def finish(got, sums, state, b, two, four):
    rows, cols = b.shape
    step = 256
    devices = got.shape[0] // 16

    def fixed(shape):
        return pl.BlockSpec(shape, lambda i: (0, 0))

    tile = pl.BlockSpec((step, cols), lambda i: (i, 0))
    small = [(1, 64), (COUNTIES // LANES, LANES), (1, 64)]
    return pl.pallas_call(
        functools.partial(finish_kernel, devices),
        grid=(rows // step,),
        out_shape=[jax.ShapeDtypeStruct(b.shape, F32)] * 2
        + [jax.ShapeDtypeStruct(shape, F32) for shape in small],
        in_specs=[fixed(got.shape), fixed(sums.shape), fixed(state.shape), tile, tile, tile],
        out_specs=[tile, tile] + [fixed(shape) for shape in small],
        scratch_shapes=[pltpu.VMEM((8, LANES), F32)],
        compiler_params=params(60),
        cost_estimate=cost(8),
        name="finish",
    )(got, sums, state, b, two, four)


def invert_pair(a, b, c):
    scale = 1.0 / (a * c - b * b)
    return c * scale, -b * scale, a * scale


def invert_block(rows):
    size = LANES
    lane, sub = iota((8, size), 1), iota((8, size), 0)
    groups = size // 8
    pivots = [jnp.ones((8, size), F32)] * groups
    for k in range(0, size, 4):
        g, s = divmod(k, 8)
        block = jnp.logical_and(lane >= k, lane < k + 4)
        factors = {
            h: [jnp.broadcast_to(rows[h][:, k + c : k + c + 1], (8, size)) for c in range(4)]
            for h in range(g, groups)
        }

        def at(i, j):
            return jnp.broadcast_to(factors[g][j][s + i : s + i + 1, :], (8, size))

        line = []
        for i in range(4):
            whole = jnp.broadcast_to(rows[g][s + i : s + i + 1, :], (8, size))
            line.append(jnp.where(block, jnp.where(lane == k + i, 1.0, 0.0), whole))
        p00, p10, p11 = at(0, 0), at(1, 0), at(1, 1)
        q00, q01, q10, q11 = at(2, 0), at(2, 1), at(3, 0), at(3, 1)
        i00, i10, i11 = invert_pair(p00, p10, p11)
        t00, t01 = q00 * i00 + q01 * i10, q00 * i10 + q01 * i11
        t10, t11 = q10 * i00 + q11 * i10, q10 * i10 + q11 * i11
        c00 = at(2, 2) - (t00 * q00 + t01 * q01)
        c10 = at(3, 2) - (t10 * q00 + t11 * q01)
        c11 = at(3, 3) - (t10 * q10 + t11 * q11)
        j00, j10, j11 = invert_pair(c00, c10, c11)
        low_2 = line[2] - (t00 * line[0] + t01 * line[1])
        low_3 = line[3] - (t10 * line[0] + t11 * line[1])
        w_2, w_3 = j00 * low_2 + j10 * low_3, j10 * low_2 + j11 * low_3
        w_0 = (i00 * line[0] + i10 * line[1]) - (t00 * w_2 + t10 * w_3)
        w_1 = (i10 * line[0] + i11 * line[1]) - (t01 * w_2 + t11 * w_3)
        for h in range(g, groups):
            f = factors[h]
            cut = (f[0] * w_0 + f[1] * w_1) + (f[2] * w_2 + f[3] * w_3)
            updated = jnp.where(block, 0.0, rows[h]) - cut
            if h > g:
                rows[h] = updated
                continue
            l10, l32 = p10 / p00, c10 / c00
            done = (line[0], line[1] - l10 * line[0], low_2, low_3 - l32 * low_2)
            diagonal = (p00, p11 - l10 * p10, c00, c11 - l32 * c10)
            own = jnp.where(sub >= s + 4, updated, rows[g])
            pivot = pivots[g]
            for i in range(4):
                own = jnp.where(sub == s + i, done[i], own)
                pivot = jnp.where(sub == s + i, diagonal[i], pivot)
            rows[g], pivots[g] = own, pivot
    out = []
    for g in range(groups):
        kept = jnp.where(lane <= sub + 8 * g, rows[g], 0.0)
        out.append(kept / jnp.sqrt(pivots[g]))
    return out


def factor_kernel(a, inverse, part, left):
    size = LANES
    part[...] = a[0:size, 0:size]
    inverse[0:size, size:] = jnp.zeros((size, size), F32)

    def body(index, carry):
        rows = [part[8 * g : 8 * g + 8, :] for g in range(size // 8)]
        rows = invert_block(rows)
        for g in range(size // 8):
            part[8 * g : 8 * g + 8, :] = rows[g]

        @pl.when(index == 0)
        def _():
            first = part[...]
            inverse[0:size, 0:size] = first
            left[...] = dot(a[size:, 0:size], first, (1, 1))
            part[...] = a[size:, size:] - dot(left[...], left[...], (1, 1))

        return carry

    lax.fori_loop(0, 2, body, 0)
    inverse[size:, size:] = part[...]
    inverse[size:, 0:size] = -dot(part[...], dot(left[...], inverse[0:size, 0:size]))


def factor(a):
    size = a.shape[0]
    half = pltpu.VMEM((LANES, LANES), F32)
    return pl.pallas_call(
        factor_kernel,
        out_shape=jax.ShapeDtypeStruct(a.shape, F32),
        in_specs=[pl.BlockSpec(memory_space=pltpu.VMEM)],
        out_specs=pl.BlockSpec(memory_space=pltpu.VMEM),
        scratch_shapes=[half, half],
        compiler_params=params(60),
        cost_estimate=cost(1),
        name="factor",
    )(a)


def split(value):
    high = value.astype(jnp.bfloat16)
    return high, (value - high.astype(F32)).astype(jnp.bfloat16)


def tile_rows(ref, index, size, count):
    parts = [
        ref[pl.ds(part * count + index, size, stride=count * (size // LANES)), :]
        for part in range(size // LANES)
    ]
    return jnp.concatenate(parts, axis=1)


def update_kernel(flags, column, column_got, wide_hbm, wide_got, inverse, schur, panel, updated, wide, other, sem):
    size = inverse.shape[0]
    count = other.shape[0]

    @pl.when(pl.program_id(0) == 0)
    def _():
        @pl.when(flags[4] > 0)
        def _():
            pltpu.make_async_copy(wide_got, wide, sem).start()

        @pl.when(flags[4] == 0)
        def _():
            pltpu.make_async_copy(wide_hbm, wide, sem).start()

        pltpu.make_async_copy(wide_hbm, wide, sem).wait()
        for index in range(count):
            high, low = split(dot(inverse[...], tile_rows(wide, index, size, count)))
            other[index, 0:size, :] = high
            other[index, size : 2 * size, :] = low
            other[index, 2 * size :, :] = high

    own = jnp.where(flags[5] > 0, column_got[0], column[0])
    own = dot(own, inverse[...], (1, 1))
    panel[0] = own
    high, low = split(own)
    lhs = jnp.concatenate([high, high, low], axis=1)
    for index in range(count):
        product = jnp.dot(lhs, other[index], preferred_element_type=F32)
        for part in range(size // LANES):
            at = pl.ds(part * count + index, size, stride=count * (size // LANES))
            updated[0, at, :] = schur[0, at, :] - product[:, part * LANES : (part + 1) * LANES]


def update(flags, column, column_got, wide, wide_got, inverse, schur):
    count_rows, size, count, _ = schur.shape
    parts = size // LANES
    flat = lane_tiles(schur)

    def step(*block):
        return pl.BlockSpec((1,) + block, lambda i: (i,) + (0,) * len(block))

    any_spec = pl.BlockSpec(memory_space=pl.ANY)
    inverse_spec = pl.BlockSpec(inverse.shape, lambda i: (0, 0))
    panel, updated = pl.pallas_call(
        update_kernel,
        grid=(count_rows,),
        out_shape=(
            jax.ShapeDtypeStruct(column.shape, F32),
            jax.ShapeDtypeStruct(flat.shape, F32),
        ),
        in_specs=[pl.BlockSpec(memory_space=pltpu.SMEM), step(size, size), step(size, size)]
        + [any_spec, any_spec, inverse_spec, step(*flat.shape[1:])],
        out_specs=(step(size, size), step(*flat.shape[1:])),
        scratch_shapes=[
            pltpu.VMEM(wide.shape, F32),
            pltpu.VMEM((count, 3 * size, size), jnp.bfloat16),
            pltpu.SemaphoreType.DMA,
        ],
        compiler_params=params(60),
        cost_estimate=cost(17),
        name="update",
    )(flags, column, column_got, wide, wide_got, inverse, flat)
    updated = updated.reshape(count_rows, size, parts, count, LANES).transpose(0, 1, 3, 2, 4)
    return panel, updated.reshape(schur.shape)


def per_device(right_side, kappa_sq, block_tract, tract_county, county_state, schur):
    n_row, n_col = lax.axis_size("row"), lax.axis_size("col")
    row, col = lax.axis_index("row"), lax.axis_index("col")
    flags = [row > 0, row < n_row - 1, col > 0, col < n_col - 1, row % 2 == 1, col % 2 == 1]
    flags = jnp.stack(flags).astype(jnp.int32)

    corner = corner_block(schur)
    steps = small_steps(n_row, n_col)
    corner = small_hop(corner, steps[0])
    near, far, left, right = edge_messages(flags, right_side, kappa_sq)
    near, far = trade(near, far, "row")
    near, far, corner = lax.optimization_barrier((near, far, corner))
    corner = small_hop(corner, steps[1])
    above, below, near, far = corner_messages(flags, near, far, left, right)
    near, far = trade(near, far, "col")
    near, far, corner = lax.optimization_barrier((near, far, corner))
    corner = small_hop(corner, steps[2])
    held, flat, near = lax.optimization_barrier((schur, lane_tiles(schur), near))
    column, wide = extract(held, flat)
    column, wide, corner = lax.optimization_barrier((column, wide, corner))
    column_got, wide_got = hop(column, "col", n_col), hop(wide, "row", n_row)
    for step in steps[3:]:
        corner = small_hop(corner, step)
    near, far, corner = lax.optimization_barrier((near, far, corner))

    tracts = jnp.concatenate([block_tract, block_tract], axis=1)
    pay, sums, two, four = raster(
        flags, right_side, kappa_sq, above, below, near, far, tracts, tract_county[:, None]
    )
    pay, column_got, wide_got = lax.optimization_barrier((pay, column_got, wide_got))
    got = exchange(pay).reshape(-1, LANES)
    stride = n_col
    while stride > 2:
        column = merge(column_got, column, "col", stride)
        stride //= 2
        column_got = hop(column, "col", stride)
    stride = n_row
    wide = merge(wide_got, wide, "row", stride)
    stride //= 2
    wide_got = hop(wide, "row", stride)
    inverse = factor(corner)
    wide_got, got, inverse, column_got = lax.optimization_barrier((wide_got, got, inverse, column_got))
    while stride > 2:
        wide = merge(wide_got, wide, "row", stride)
        stride //= 2
        wide_got = hop(wide, "row", stride)
    solution, residual, tract_totals, county_totals, state_totals = finish(
        got,
        sums,
        county_state.reshape(COUNTIES // LANES, LANES),
        right_side,
        two,
        four,
    )
    panel, updated = update(flags, column, column_got, wide, wide_got, inverse, schur)
    return (
        solution,
        residual,
        tract_totals.reshape(-1)[:TRACTS_DEV],
        county_totals.reshape(-1),
        state_totals.reshape(-1)[:STATES],
        updated,
        panel,
    )


def solution(mesh):
    in_specs = (
        P("row", "col"),
        P("row", "col"),
        P("row", "col"),
        P(("row", "col")),
        P(),
        P(None, "row", None, "col"),
    )
    out_specs = (
        P("row", "col"),
        P("row", "col"),
        P(("row", "col")),
        P(),
        P(),
        P(None, "row", None, "col"),
        P(None, "row", None),
    )
    return jax.shard_map(
        per_device, mesh=mesh, in_specs=in_specs, out_specs=out_specs, check_vma=False
    )
```
